32 devices in a mesh: slab: 8 (over z, x), row: 4 (over y, core).
Axes of the slice: x: 2, y: 2, z: 4, core: 2. Of those that a mesh axis runs over, the one named last changes fastest.
Arguments:
- edge_weights: int32 [3, 16, 32, 512], P(None, 'slab', 'row'), may hold values from 1 to 15
- seeds: int32 [16, 32, 512], P('slab', 'row'), may hold values from -8 to 7
- supervoxel: int32 [16, 32, 512], P('slab', 'row'), may hold values from 0 to 127
- coarse_blocks: float32 [4, 1024, 1024], P('row', 'slab'), as said below
Outputs:
- potentials: float32 [8, 16, 32, 512], P(None, 'slab', 'row')
The draws below stay inside these ranges and needn't reach their ends.
Inputs may be any that keep to these rules, and one draw needn't show every extreme that they name: `seeds`: a negative value marks an unseeded voxel. `coarse_blocks`: the entries named by dc lie between 0.6 and 1.2 times 2 * 8 * 4.
All inputs are finite; a program needn't handle non-finite values.
Results may differ from the reference program's by a relative error of at most 0.00024.
Values sent between devices are 32-bit elements; how exact they have to be, the bound alone decides.
No kernel may reach another device: no remote copies, remote signals or barrier semaphores. Data moves between devices by JAX's collectives and lax.ppermute only.
A program may use at most 64 MiB of HBM per device.

```python
import jax
import jax.numpy as jnp
from jax import lax

LABELS = 8
CZ = 2
CY = 8
NX = 512
CC = 128
CYCLES = 2
GROUP = 8
SECTIONS = 1
NZ = 16
NY = 32
N_SLAB = 8
N_ROW = 4


def draw_coarse_blocks(key, part):
    shape = (N_ROW, N_SLAB * CC, GROUP * CC)
    first_key, second_key, third_key = jax.random.split(jax.random.fold_in(key, 7), 3)
    volume_share = CZ * CY * NX / CC
    sections = N_SLAB // GROUP
    rows = lax.broadcasted_iota(jnp.int32, shape, 1)
    columns = lax.broadcasted_iota(jnp.int32, shape, 2)
    device = rows // CC
    member = device // sections
    on_main = columns == member * CC + rows % CC
    partner_shift = jax.random.randint(third_key, (N_ROW, N_SLAB), 1, GROUP)
    member_ids = jnp.arange(N_SLAB, dtype=jnp.int32) // sections
    partner = (member_ids[None, :] + partner_shift) % GROUP
    partner_full = jnp.repeat(partner, CC, axis=1)[:, :, None]
    heavy = (columns // CC == partner_full).astype(jnp.float32)
    uniform_part = jax.random.uniform(first_key, shape, jnp.float32, 0.0, 1.0)
    spread = 2.0 * uniform_part
    base = 0.5 * volume_share / ((GROUP + 6) * CC)
    off_values = -base * spread * (1.0 + 6.0 * heavy)
    main_values = volume_share * jax.random.uniform(second_key, shape[:2], jnp.float32, 0.6, 1.2)
    return jnp.where(on_main, main_values[:, :, None], off_values)


def place_ends(values, own_key, smallest, top_value):
    shape = values.shape
    place = [jax.random.randint(jax.random.fold_in(own_key, axis), (), 0, shape[axis]) for axis in range(len(shape))]
    values = values.at[tuple(place)].set(smallest)
    longest = shape.index(max(shape))
    place[longest] = (place[longest] + 1) % shape[longest]
    return values.at[tuple(place)].set(top_value)


def setup_inputs(seed: int = 0) -> dict:
    splits = jax.random.split(jax.random.key(seed), 5)
    edge_weights = place_ends(jax.random.randint(splits[0], (3, NZ, NY, NX), 1, 16), jax.random.fold_in(splits[0], 1), 1, 15).astype(jnp.int32)
    seeds = place_ends(jax.random.randint(splits[1], (NZ, NY, NX), -8, 8), jax.random.fold_in(splits[1], 1), -8, 7).astype(jnp.int32)
    supervoxel = place_ends(jax.random.randint(splits[2], (NZ, NY, NX), 0, CC), jax.random.fold_in(splits[2], 1), 0, CC - 1).astype(jnp.int32)
    coarse_blocks = draw_coarse_blocks(jax.random.fold_in(splits[4], 71), 0)
    return {"edge_weights": edge_weights, "seeds": seeds, "supervoxel": supervoxel, "coarse_blocks": coarse_blocks}


prior_mass = 0.25
seed_weight = 4.0
smooth_step = 0.8
coarse_step = 0.7
weight_unit = 0.125


def lower_value(a, axis):
    pads = [(0, 0)] * a.ndim
    pads[axis] = (1, 0)
    return jnp.pad(lax.slice_in_dim(a, 0, a.shape[axis] - 1, axis=axis), pads)


def upper_value(a, axis):
    pads = [(0, 0)] * a.ndim
    pads[axis] = (0, 1)
    return jnp.pad(lax.slice_in_dim(a, 1, a.shape[axis], axis=axis), pads)


def reference(edge_weights, seeds, supervoxel, coarse_blocks):
    weights = edge_weights.astype(jnp.float32) * weight_unit
    keep_z = (jnp.arange(NZ) < NZ - 1).astype(jnp.float32)[:, None, None]
    keep_y = (jnp.arange(NY) < NY - 1).astype(jnp.float32)[None, :, None]
    keep_x = (jnp.arange(NX) < NX - 1).astype(jnp.float32)[None, None, :]
    w_z = weights[0] * keep_z
    w_y = weights[1] * keep_y
    w_x = weights[2] * keep_x
    below_z = lower_value(w_z, 0)
    below_y = lower_value(w_y, 1)
    below_x = lower_value(w_x, 2)
    seeded = (seeds >= 0).astype(jnp.float32)
    diag = prior_mass + seed_weight * seeded + w_z + w_y + w_x + below_z + below_y + below_x
    label_ids = jnp.arange(LABELS, dtype=jnp.int32)
    source = seed_weight * (seeds[None] == label_ids[:, None, None, None]).astype(jnp.float32)

    def operate(field):
        near = w_z * upper_value(field, 1) + below_z * lower_value(field, 1)
        near = near + w_y * upper_value(field, 2) + below_y * lower_value(field, 2)
        near = near + w_x * upper_value(field, 3) + below_x * lower_value(field, 3)
        return diag * field - near

    def sweep(field):
        return field + smooth_step * (source - operate(field)) / diag

    owner_z = jnp.arange(NZ, dtype=jnp.int32) // CZ
    owner_y = jnp.arange(NY, dtype=jnp.int32) // CY
    owner = owner_y[None, :] * N_SLAB + owner_z[:, None]
    global_ids = (owner[:, :, None] * CC + supervoxel).reshape(-1)
    segments = N_ROW * N_SLAB * CC
    blocks_four = coarse_blocks.reshape(N_ROW, N_SLAB, CC, GROUP, CC)
    diag_all = jnp.diagonal(blocks_four, axis1=2, axis2=4)
    member_of = jnp.arange(N_SLAB, dtype=jnp.int32) // SECTIONS
    picker = (jnp.arange(GROUP, dtype=jnp.int32)[None, :] == member_of[:, None]).astype(jnp.float32)
    coarse_diag = jnp.sum(diag_all * picker[None, :, :, None], axis=2)
    blocks_six = coarse_blocks.reshape(N_ROW, GROUP, SECTIONS, CC, GROUP, CC)

    field = jnp.zeros((LABELS, NZ, NY, NX), jnp.float32)
    for cycle in range(CYCLES):
        field = sweep(sweep(field))
        residual = source - operate(field)
        summed = jax.ops.segment_sum(residual.reshape(LABELS, -1).T, global_ids, num_segments=segments)
        coarse_rhs = summed.T.reshape(LABELS, N_ROW, N_SLAB, CC)
        first = coarse_step * coarse_rhs / coarse_diag
        vector = first.reshape(LABELS, N_ROW, GROUP, SECTIONS, CC)
        applied = jnp.einsum("qtgaub,lqugb->lqtga", blocks_six, vector, precision=lax.Precision.HIGHEST)
        applied = applied.reshape(LABELS, N_ROW, N_SLAB, CC)
        second = first + coarse_step * (coarse_rhs - applied) / coarse_diag
        correction = jnp.take(second.reshape(LABELS, segments), global_ids, axis=1)
        field = field + correction.reshape(LABELS, NZ, NY, NX)
        field = sweep(field)
    return field
```

```python
import math

import jax
import jax.numpy as jnp
from jax import lax
from jax.experimental import pallas as pl
from jax.experimental.pallas import tpu as pltpu
from jax.sharding import PartitionSpec as P

LABELS = 8
CYCLES = 2

prior_mass = 0.25
seed_weight = 4.0
smooth_step = 0.8
coarse_step = 0.7
weight_unit = 0.125

BOTH = ("slab", "row")
NEED = 5
VMEM_LIMIT = 60 * 1024 * 1024


def pairing(n_slab, n_row, axis, distance, phase):
    count = n_slab if axis == "slab" else n_row
    spare = n_row if axis == "slab" else n_slab
    pairs = []
    for s in range(n_slab):
        for r in range(n_row):
            i, other = (s, r) if axis == "slab" else (r, s)
            if (i // distance) % 2 == phase and i + distance < count:
                j, k = i + distance, other
            elif i >= distance and (i // distance - 1) % 2 == phase:
                j, k = i - distance, other
            elif spare % 2 == 0:
                j, k = i, other ^ 1
            else:
                continue
            target = (j, k) if axis == "slab" else (k, j)
            pairs.append((s * n_row + r, target[0] * n_row + target[1]))
    return pairs


def swap(block, axis, distance, phase):
    n_slab, n_row = lax.axis_size("slab"), lax.axis_size("row")
    return lax.ppermute(block, BOTH, pairing(n_slab, n_row, axis, distance, phase))


def vmem(count):
    return [pl.BlockSpec(memory_space=pltpu.VMEM)] * count


def params():
    return pltpu.CompilerParams(vmem_limit_bytes=VMEM_LIMIT)


class Shape:
    def __init__(self, edge_weights, coarse_blocks):
        self.cz, self.cy, self.nx = edge_weights.shape[1:]
        self.cc = coarse_blocks.shape[1]
        self.group = coarse_blocks.shape[2] // self.cc
        self.n_slab = lax.axis_size("slab")
        self.n_row = lax.axis_size("row")
        self.sections = self.n_slab // self.group
        self.reach = -(-(NEED + 1) // self.cz)
        self.oz = self.reach * self.cz
        self.planes = self.cz + 2 * self.oz
        self.rows = 3 * self.cy
        self.oy = self.cy

    def away(self, z):
        return -z if z < 0 else max(0, z - self.cz + 1)

    def strips(self):
        out, at = [], 0
        for z in range(-self.oz, self.cz + self.oz):
            take = NEED + 1 - self.away(z)
            if take > 0:
                out.append((z, at, take))
                at += take
        return out, -(-at // 8) * 8


def parity_of(index, distance):
    return (index // distance) % 2


def pack_kernel(shape, own_ref, *refs):
    recvs, (frame_ref, even_ref, odd_ref) = refs[:-3], refs[-3:]
    cz, oz = shape.cz, shape.oz
    slab = lax.axis_index("slab")
    row = lax.axis_index("row")
    for a in range(5):
        for z in range(cz):
            frame_ref[a, oz + z] = own_ref[a, z]
    for d in range(1, shape.reach + 1):
        first, second = recvs[2 * d - 2], recvs[2 * d - 1]
        par = parity_of(slab, d)

        def place(above, below, d=d):
            for a in range(5):
                for z in range(cz):
                    frame_ref[a, oz + d * cz + z] = above[a, z]
                    frame_ref[a, oz - d * cz + z] = below[a, z]

        @pl.when(par == 0)
        def _():
            place(first, second)

        @pl.when(par == 1)
        def _():
            place(second, first)

    strips, _ = shape.strips()

    def fill(last_ref, first_ref):
        for z, at, take in strips:
            for a in range(5):
                tile = frame_ref[a, oz + z]
                last_ref[a, at : at + take] = tile[shape.cy - take :]
                first_ref[a, at : at + take] = tile[:take]

    @pl.when(row % 2 == 0)
    def _():
        fill(even_ref, odd_ref)

    @pl.when(row % 2 == 1)
    def _():
        fill(odd_ref, even_ref)


def row_of(ref, z, y, count):
    return jnp.broadcast_to(ref[z, y : y + 1, :], (LABELS, count))


class Fields:
    def __init__(self, shape, wz, wy, wx, wxl, k, seeds):
        self.s = shape
        self.wz, self.wy, self.wx, self.wxl, self.k, self.seeds = wz, wy, wx, wxl, k, seeds
        self.lab = lax.broadcasted_iota(jnp.int32, (LABELS, shape.nx), 0)

    def region(self, layers, body):
        s = self.s
        for m in range(layers + 1):
            lo, hi = -(layers - m), s.cy + layers - m
            if m == 0:
                def inner(i, c, lo=lo, hi=hi):
                    body(i, lo, hi)
                    return c

                lax.fori_loop(0, s.cz, inner, 0)
            else:
                def inner(i, c, m=m, lo=lo, hi=hi):
                    body(jnp.where(i == 0, -m, s.cz - 1 + m), lo, hi)
                    return c

                lax.fori_loop(0, 2, inner, 0)

    def source(self, z, y):
        s = self.s
        seeds = row_of(self.seeds, z + s.oz, y + s.oy, s.nx)
        return jnp.where(seeds == self.lab, seed_weight, 0.0)

    def near_rows(self, src, pz, py, z, lo, hi, use):
        s = self.s
        zz = z + s.oz
        before = src[z + pz, lo - 1 + py]
        centre = src[z + pz, lo + py]
        w_before = row_of(self.wy, zz, lo - 1 + s.oy, s.nx)
        for y in range(lo, hi):
            yy = y + s.oy
            after = src[z + pz, y + 1 + py]
            w_after = row_of(self.wy, zz, yy, s.nx)
            near = row_of(self.wz, zz, yy, s.nx) * src[z + 1 + pz, y + py]
            near = near + row_of(self.wz, zz - 1, yy, s.nx) * src[z - 1 + pz, y + py]
            near = near + w_after * after + w_before * before
            near = near + row_of(self.wx, zz, yy, s.nx) * pltpu.roll(centre, s.nx - 1, axis=1)
            near = near + row_of(self.wxl, zz, yy, s.nx) * pltpu.roll(centre, 1, axis=1)
            use(y, centre, near)
            before, centre, w_before = centre, after, w_after

    def sweep(self, src, src_at, dst, dst_at, layers):
        s = self.s

        def body(z, lo, hi):
            def use(y, centre, near):
                k = row_of(self.k, z + s.oz, y + s.oy, s.nx)
                dst[z + dst_at[0], y + dst_at[1]] = (1.0 - smooth_step) * centre + k * (
                    self.source(z, y) + near
                )

            self.near_rows(src, *src_at, z, lo, hi, use)

        self.region(layers, body)

    def coarse_sums(self, src, src_at, diag, diag_z, owners, acc):
        s = self.s
        acc[...] = jnp.zeros_like(acc)
        cells = lax.broadcasted_iota(jnp.int32, (s.cc, s.nx), 0)

        def body(z, lo, hi):
            def use(y, centre, near):
                d = row_of(diag, z + diag_z, y + s.oy, s.nx)
                rest = self.source(z, y) - (d * centre - near)
                top = rest.astype(jnp.bfloat16).astype(jnp.float32)
                mid = (rest - top).astype(jnp.bfloat16).astype(jnp.float32)
                low = rest - top - mid
                parts = jnp.concatenate([top, mid, low], axis=0).astype(jnp.bfloat16)
                ids = jnp.broadcast_to(owners[z + s.oz, y + s.oy : y + s.oy + 1, :], (s.cc, s.nx))
                onehot = jnp.where(ids == cells, 1.0, 0.0).astype(jnp.bfloat16)
                acc[...] += lax.dot_general(
                    parts, onehot, (((1,), (1,)), ((), ())), preferred_element_type=jnp.float32
                )

            self.near_rows(src, *src_at, z, lo, hi, use)

        self.region(0, body)
        return acc[0:LABELS] + acc[LABELS : 2 * LABELS] + acc[2 * LABELS : 3 * LABELS]


def take(table, ids, shape):
    ids = jnp.broadcast_to(ids, (LABELS, shape.nx))
    parts = [
        jnp.take_along_axis(table, ids[:, i : i + shape.cc], axis=1, mode="promise_in_bounds")
        for i in range(0, shape.nx, shape.cc)
    ]
    return jnp.concatenate(parts, axis=1)


def own_diagonal(blocks_ref, shape):
    turn = lax.axis_index("slab") // shape.sections
    own = blocks_ref[:, pl.ds(pl.multiple_of(turn * shape.cc, shape.cc), shape.cc)]
    a = lax.broadcasted_iota(jnp.int32, own.shape, 0)
    b = lax.broadcasted_iota(jnp.int32, own.shape, 1)
    return jnp.sum(jnp.where(a == b, own, 0.0), axis=0, keepdims=True)


def down_kernel(shape, frame_ref, even_ref, odd_ref, blocks_ref, *refs):
    (wz, wy, wx, wxl, k, seeds, owners, diag, u2, rhs_ref, first_ref, ints, u1, acc) = refs
    s = shape
    slab = lax.axis_index("slab")
    row = lax.axis_index("row")
    cy, oy, oz = s.cy, s.oy, s.oz
    strips, _ = s.strips()

    def sides(below_ref, above_ref):
        for z, at, count in strips:
            for a in range(5):
                ints[a, oz + z, oy - count : oy] = below_ref[a, at : at + count]
                ints[a, oz + z, oy + cy : oy + cy + count] = above_ref[a, at : at + count]

    @pl.when(row % 2 == 0)
    def _():
        sides(odd_ref, even_ref)

    @pl.when(row % 2 == 1)
    def _():
        sides(even_ref, odd_ref)

    def prepare(i, lower_wz):
        for a in range(5):
            ints[a, i, oy : oy + cy] = frame_ref[a, i]
        plane = slab * s.cz + i - oz
        line = row * cy - oy + lax.broadcasted_iota(jnp.int32, (s.rows, s.nx), 0)
        column = lax.broadcasted_iota(jnp.int32, (s.rows, s.nx), 1)
        keep_plane = jnp.logical_and(plane != -1, plane != s.cz * s.n_slab - 1)
        keep_line = jnp.logical_and(line != -1, line != cy * s.n_row - 1)
        w_z = ints[0, i].astype(jnp.float32) * jnp.where(keep_plane, weight_unit, 0.0)
        w_y = jnp.where(keep_line, ints[1, i].astype(jnp.float32) * weight_unit, 0.0)
        w_x = jnp.where(column < s.nx - 1, ints[2, i].astype(jnp.float32) * weight_unit, 0.0)
        w_xl = pltpu.roll(w_x, 1, axis=1)
        seed = ints[3, i]
        d = (
            prior_mass
            + seed_weight * (seed >= 0).astype(jnp.float32)
            + w_z
            + w_y
            + w_x
            + lower_wz
            + pltpu.roll(w_y, 1, axis=0)
            + w_xl
        )
        wz[i] = w_z
        wy[i] = w_y
        wx[i] = w_x
        wxl[i] = w_xl
        k[i] = smooth_step / d
        diag[i] = d
        seeds[i] = seed
        owners[i] = ints[4, i]
        return w_z

    lax.fori_loop(0, s.planes, prepare, jnp.zeros((s.rows, s.nx), jnp.float32))
    fields = Fields(s, wz, wy, wx, wxl, k, seeds)
    at1 = (NEED, NEED)

    def start(z, lo, hi):
        for y in range(lo, hi):
            kk = row_of(k, z + oz, y + oy, s.nx)
            seed = row_of(seeds, z + oz, y + oy, s.nx)
            u1[z + at1[0], y + at1[1]] = jnp.where(seed == fields.lab, seed_weight * kk, 0.0)

    fields.region(NEED, start)
    at2 = (NEED - 1, NEED - 1)
    fields.sweep(u1, at1, u2, at2, NEED - 1)
    rhs = fields.coarse_sums(u2, at2, diag, oz, owners, acc)
    rhs_ref[...] = rhs
    first = coarse_step * rhs / own_diagonal(blocks_ref, s)
    for t in range(s.group):
        first_ref[t] = first


def coarse_kernel(shape, first_ref, rhs_ref, blocks_ref, second_ref):
    s = shape
    turn = lax.axis_index("slab") // s.sections
    mine = first_ref[turn]
    whole = jnp.concatenate([first_ref[t] for t in range(s.group)], axis=1)
    applied = lax.dot_general(
        whole,
        blocks_ref[...],
        (((1,), (1,)), ((), ())),
        precision=lax.Precision.HIGHEST,
        preferred_element_type=jnp.float32,
    )
    second = mine + coarse_step * (rhs_ref[...] - applied) / own_diagonal(blocks_ref, s)
    for i in range(second_ref.shape[0]):
        second_ref[i] = second


def middle_kernel(shape, second_ref, blocks_ref, wz, wy, wx, wxl, k, seeds, owners, diag, u2, *refs):
    (u5, rhs_ref, first_ref, u3, u4, acc) = refs
    s = shape
    slab = lax.axis_index("slab")
    row = lax.axis_index("row")
    fields = Fields(s, wz, wy, wx, wxl, k, seeds)
    layers = NEED - 1
    at2 = (layers, layers)

    def table(dz, dy):
        i = jnp.clip(slab + dz, 0, s.n_slab - 1) * s.n_row + jnp.clip(row + dy, 0, s.n_row - 1)
        return second_ref[i]

    def correct(z, lo, hi):
        dz = lax.div(z + s.oz, s.cz) - s.reach
        for dy in (-1, 0, 1):
            begin, end = max(lo, dy * s.cy), min(hi, (dy + 1) * s.cy)
            if begin >= end:
                continue
            tab = table(dz, dy)
            for y in range(begin, end):
                ids = owners[z + s.oz, y + s.oy : y + s.oy + 1, :]
                at = (z + at2[0], y + at2[1])
                u4[at] = u2[at] + take(tab, ids, s)

    fields.region(layers, correct)
    fields.sweep(u4, at2, u3, at2, layers - 1)
    fields.sweep(u3, at2, u4, at2, layers - 2)
    fields.sweep(u4, at2, u5, (1, 1), 1)
    rhs = fields.coarse_sums(u5, (1, 1), diag, s.oz, owners, acc)
    rhs_ref[...] = rhs
    first = coarse_step * rhs / own_diagonal(blocks_ref, s)
    for t in range(s.group):
        first_ref[t] = first


def last_kernel(shape, own_ref, z0, z1, y0, y1, wz, wy, wx, wxl, k, seeds, owners, u5, out_ref, u6):
    s = shape
    slab = lax.axis_index("slab")
    row = lax.axis_index("row")
    fields = Fields(s, wz, wy, wx, wxl, k, seeds)

    def pick(even, first, second):
        return jnp.where(even, first[0], second[0])

    up_z = pick(slab % 2 == 0, z0, z1)
    down_z = pick(slab % 2 == 0, z1, z0)
    up_y = pick(row % 2 == 0, y0, y1)
    down_y = pick(row % 2 == 0, y1, y0)

    def add(z, y, tab):
        ids = owners[z + s.oz, y + s.oy : y + s.oy + 1, :]
        u6[z + 1, y + 1] = u5[z + 1, y + 1] + take(tab, ids, s)

    own = own_ref[0]
    for y in range(s.cy):
        add(-1, y, down_z)
        add(s.cz, y, up_z)

    def plane(z, c):
        add(z, -1, down_y)
        add(z, s.cy, up_y)
        for y in range(s.cy):
            add(z, y, own)
        return c

    lax.fori_loop(0, s.cz, plane, 0)

    def body(z, lo, hi):
        def use(y, centre, near):
            kk = row_of(k, z + s.oz, y + s.oy, s.nx)
            out_ref[:, z, y, :] = (1.0 - smooth_step) * centre + kk * (fields.source(z, y) + near)

        fields.near_rows(u6, 1, 1, z, lo, hi, use)

    fields.region(0, body)


def f32(*dims):
    return jax.ShapeDtypeStruct(dims, jnp.float32)


def i32(*dims):
    return jax.ShapeDtypeStruct(dims, jnp.int32)


def per_device(edge_weights, seeds, supervoxel, coarse_blocks):
    import functools

    s = Shape(edge_weights, coarse_blocks)
    blocks = coarse_blocks[0]
    own = jnp.concatenate([edge_weights, seeds[None], supervoxel[None]], axis=0)
    recvs = [swap(own, "slab", d, ph) for d in range(1, s.reach + 1) for ph in (0, 1)]
    _, packed = s.strips()
    frame, even, odd = pl.pallas_call(
        functools.partial(pack_kernel, s),
        out_shape=(i32(5, s.planes, s.cy, s.nx), i32(5, packed, s.nx), i32(5, packed, s.nx)),
        in_specs=vmem(1 + len(recvs)),
        out_specs=tuple(vmem(3)),
        compiler_params=params(),
        name="pack",
    )(own, *recvs)
    even = swap(even, "row", 1, 0)
    odd = swap(odd, "row", 1, 1)
    plane = (s.planes, s.rows, s.nx)
    wide = 2 * (NEED - 1)
    *kept, u2, rhs, first = pl.pallas_call(
        functools.partial(down_kernel, s),
        out_shape=tuple(
            [f32(*plane)] * 5
            + [i32(*plane)] * 2
            + [f32(*plane), f32(s.cz + wide, s.cy + wide, LABELS, s.nx)]
            + [f32(LABELS, s.cc), f32(s.group, LABELS, s.cc)]
        ),
        in_specs=vmem(4),
        out_specs=tuple(vmem(11)),
        scratch_shapes=[
            pltpu.VMEM((5,) + plane, jnp.int32),
            pltpu.VMEM((s.cz + 2 * NEED, s.cy + 2 * NEED, LABELS, s.nx), jnp.float32),
            pltpu.VMEM((3 * LABELS, s.cc), jnp.float32),
        ],
        compiler_params=params(),
        name="down",
    )(frame, even, odd, blocks)
    diag = kept[7]

    groups = [[t * s.sections + g for t in range(s.group)] for g in range(s.sections)]

    def coarse(first, rhs, copies):
        gathered = lax.all_to_all(
            first, "slab", 0, 0, axis_index_groups=groups if s.sections > 1 else None, tiled=True
        )
        return pl.pallas_call(
            functools.partial(coarse_kernel, s),
            out_shape=f32(copies, LABELS, s.cc),
            in_specs=vmem(3),
            out_specs=vmem(1)[0],
            compiler_params=params(),
            name="coarse",
        )(gathered, rhs, blocks)

    second = coarse(first, rhs, s.n_slab * s.n_row)
    second = lax.all_to_all(second, BOTH, 0, 0, tiled=True)
    u5, rhs, first = pl.pallas_call(
        functools.partial(middle_kernel, s),
        out_shape=(
            f32(s.cz + 2, s.cy + 2, LABELS, s.nx),
            f32(LABELS, s.cc),
            f32(s.group, LABELS, s.cc),
        ),
        in_specs=vmem(11),
        out_specs=tuple(vmem(3)),
        scratch_shapes=[
            pltpu.VMEM((s.cz + wide, s.cy + wide, LABELS, s.nx), jnp.float32),
            pltpu.VMEM((s.cz + wide, s.cy + wide, LABELS, s.nx), jnp.float32),
            pltpu.VMEM((3 * LABELS, s.cc), jnp.float32),
        ],
        compiler_params=params(),
        name="middle",
    )(second, blocks, *kept[:7], diag, u2)
    second = coarse(first, rhs, 1)
    around = [swap(second, axis, 1, ph) for axis in ("slab", "row") for ph in (0, 1)]
    return pl.pallas_call(
        functools.partial(last_kernel, s),
        out_shape=f32(LABELS, s.cz, s.cy, s.nx),
        in_specs=vmem(13),
        out_specs=vmem(1)[0],
        scratch_shapes=[pltpu.VMEM((s.cz + 2, s.cy + 2, LABELS, s.nx), jnp.float32)],
        compiler_params=params(),
        name="last",
    )(second, *around, *kept[:7], u5)


def solution(mesh):
    in_specs = (
        P(None, "slab", "row", None),
        P("slab", "row", None),
        P("slab", "row", None),
        P("row", "slab", None),
    )
    out_specs = P(None, "slab", "row", None)
    return jax.shard_map(
        per_device, mesh=mesh, in_specs=in_specs, out_specs=out_specs, check_vma=False
    )
```

```python
import math

import jax
import jax.numpy as jnp
from jax import lax
from jax.experimental import pallas as pl
from jax.experimental.pallas import tpu as pltpu
from jax.sharding import PartitionSpec as P

LABELS = 8
CYCLES = 2

prior_mass = 0.25
seed_weight = 4.0
smooth_step = 0.8
coarse_step = 0.7
weight_unit = 0.125

BOTH = ("slab", "row")
NEED = 5
VMEM_LIMIT = 24 * 1024 * 1024


def pairing(n_slab, n_row, axis, distance, phase):
    count = n_slab if axis == "slab" else n_row
    spare = n_row if axis == "slab" else n_slab
    pairs = []
    for s in range(n_slab):
        for r in range(n_row):
            i, other = (s, r) if axis == "slab" else (r, s)
            if (i // distance) % 2 == phase and i + distance < count:
                j, k = i + distance, other
            elif i >= distance and (i // distance - 1) % 2 == phase:
                j, k = i - distance, other
            elif spare % 2 == 0:
                j, k = i, other ^ 1
            else:
                continue
            target = (j, k) if axis == "slab" else (k, j)
            pairs.append((s * n_row + r, target[0] * n_row + target[1]))
    return pairs


def swap(block, axis, distance, phase):
    n_slab, n_row = lax.axis_size("slab"), lax.axis_size("row")
    return lax.ppermute(block, BOTH, pairing(n_slab, n_row, axis, distance, phase))


def vmem(count):
    return [pl.BlockSpec(memory_space=pltpu.VMEM)] * count


def params():
    return pltpu.CompilerParams(vmem_limit_bytes=VMEM_LIMIT)


class Shape:
    def __init__(self, edge_weights, coarse_blocks):
        self.cz, self.cy, self.nx = edge_weights.shape[1:]
        self.cc = coarse_blocks.shape[1]
        self.group = coarse_blocks.shape[2] // self.cc
        self.n_slab = lax.axis_size("slab")
        self.n_row = lax.axis_size("row")
        self.sections = self.n_slab // self.group
        self.reach = -(-(NEED + 1) // self.cz)
        self.oz = self.reach * self.cz
        self.planes = self.cz + 2 * self.oz
        self.rows = 3 * self.cy
        self.oy = self.cy

    def away(self, z):
        return -z if z < 0 else max(0, z - self.cz + 1)

    def strips(self):
        out, at = [], 0
        for z in range(-self.oz, self.cz + self.oz):
            take = NEED + 1 - self.away(z)
            if take > 0:
                out.append((z, at, take))
                at += take
        return out, -(-at // 8) * 8


def parity_of(index, distance):
    return (index // distance) % 2


def pack_kernel(shape, own_ref, *refs):
    recvs, (frame_ref, even_ref, odd_ref) = refs[:-3], refs[-3:]
    cz, oz = shape.cz, shape.oz
    slab = lax.axis_index("slab")
    row = lax.axis_index("row")
    for a in range(5):
        for z in range(cz):
            frame_ref[a, oz + z] = own_ref[a, z]
    for d in range(1, shape.reach + 1):
        first, second = recvs[2 * d - 2], recvs[2 * d - 1]
        par = parity_of(slab, d)

        def place(above, below, d=d):
            for a in range(5):
                for z in range(cz):
                    frame_ref[a, oz + d * cz + z] = above[a, z]
                    frame_ref[a, oz - d * cz + z] = below[a, z]

        @pl.when(par == 0)
        def _():
            place(first, second)

        @pl.when(par == 1)
        def _():
            place(second, first)

    strips, _ = shape.strips()

    def fill(last_ref, first_ref):
        for z, at, take in strips:
            for a in range(5):
                tile = frame_ref[a, oz + z]
                last_ref[a, at : at + take] = tile[shape.cy - take :]
                first_ref[a, at : at + take] = tile[:take]

    @pl.when(row % 2 == 0)
    def _():
        fill(even_ref, odd_ref)

    @pl.when(row % 2 == 1)
    def _():
        fill(odd_ref, even_ref)


def row_of(ref, z, y, count):
    return jnp.broadcast_to(ref[z, y : y + 1, :], (LABELS, count))


class Fields:
    def __init__(self, shape, wz, wy, wx, wxl, k, seeds):
        self.s = shape
        self.wz, self.wy, self.wx, self.wxl, self.k, self.seeds = wz, wy, wx, wxl, k, seeds
        self.lab = lax.broadcasted_iota(jnp.int32, (LABELS, shape.nx), 0)

    def region(self, layers, body):
        s = self.s
        for m in range(layers + 1):
            lo, hi = -(layers - m), s.cy + layers - m
            if m == 0:
                def inner(i, c, lo=lo, hi=hi):
                    body(i, lo, hi)
                    return c

                lax.fori_loop(0, s.cz, inner, 0)
            else:
                def inner(i, c, m=m, lo=lo, hi=hi):
                    body(jnp.where(i == 0, -m, s.cz - 1 + m), lo, hi)
                    return c

                lax.fori_loop(0, 2, inner, 0)

    def source(self, z, y):
        s = self.s
        seeds = row_of(self.seeds, z + s.oz, y + s.oy, s.nx)
        return jnp.where(seeds == self.lab, seed_weight, 0.0)

    def near_rows(self, src, pz, py, z, lo, hi, use):
        s = self.s
        zz = z + s.oz
        before = src[z + pz, lo - 1 + py]
        centre = src[z + pz, lo + py]
        w_before = row_of(self.wy, zz, lo - 1 + s.oy, s.nx)
        for y in range(lo, hi):
            yy = y + s.oy
            after = src[z + pz, y + 1 + py]
            w_after = row_of(self.wy, zz, yy, s.nx)
            near = row_of(self.wz, zz, yy, s.nx) * src[z + 1 + pz, y + py]
            near = near + row_of(self.wz, zz - 1, yy, s.nx) * src[z - 1 + pz, y + py]
            near = near + w_after * after + w_before * before
            near = near + row_of(self.wx, zz, yy, s.nx) * pltpu.roll(centre, s.nx - 1, axis=1)
            near = near + row_of(self.wxl, zz, yy, s.nx) * pltpu.roll(centre, 1, axis=1)
            use(y, centre, near)
            before, centre, w_before = centre, after, w_after

    def sweep(self, src, src_at, dst, dst_at, layers):
        s = self.s

        def body(z, lo, hi):
            def use(y, centre, near):
                k = row_of(self.k, z + s.oz, y + s.oy, s.nx)
                dst[z + dst_at[0], y + dst_at[1]] = (1.0 - smooth_step) * centre + k * (
                    self.source(z, y) + near
                )

            self.near_rows(src, *src_at, z, lo, hi, use)

        self.region(layers, body)

    def coarse_sums(self, src, src_at, diag, diag_z, owners, acc):
        s = self.s
        acc[...] = jnp.zeros_like(acc)
        cells = lax.broadcasted_iota(jnp.int32, (s.cc, s.nx), 0)

        def body(z, lo, hi):
            def use(y, centre, near):
                d = row_of(diag, z + diag_z, y + s.oy, s.nx)
                rest = self.source(z, y) - (d * centre - near)
                top = rest.astype(jnp.bfloat16).astype(jnp.float32)
                mid = (rest - top).astype(jnp.bfloat16).astype(jnp.float32)
                low = rest - top - mid
                parts = jnp.concatenate([top, mid, low], axis=0).astype(jnp.bfloat16)
                ids = jnp.broadcast_to(owners[z + s.oz, y + s.oy : y + s.oy + 1, :], (s.cc, s.nx))
                onehot = jnp.where(ids == cells, 1.0, 0.0).astype(jnp.bfloat16)
                acc[...] += lax.dot_general(
                    parts, onehot, (((1,), (1,)), ((), ())), preferred_element_type=jnp.float32
                )

            self.near_rows(src, *src_at, z, lo, hi, use)

        self.region(0, body)
        return acc[0:LABELS] + acc[LABELS : 2 * LABELS] + acc[2 * LABELS : 3 * LABELS]


def take(table, ids, shape):
    ids = jnp.broadcast_to(ids, (LABELS, shape.nx))
    parts = [
        jnp.take_along_axis(table, ids[:, i : i + shape.cc], axis=1, mode="promise_in_bounds")
        for i in range(0, shape.nx, shape.cc)
    ]
    return jnp.concatenate(parts, axis=1)


def own_diagonal(blocks_ref, shape):
    turn = lax.axis_index("slab") // shape.sections
    own = blocks_ref[:, pl.ds(pl.multiple_of(turn * shape.cc, shape.cc), shape.cc)]
    a = lax.broadcasted_iota(jnp.int32, own.shape, 0)
    b = lax.broadcasted_iota(jnp.int32, own.shape, 1)
    return jnp.sum(jnp.where(a == b, own, 0.0), axis=0, keepdims=True)


def down_kernel(shape, frame_ref, even_ref, odd_ref, blocks_ref, *refs):
    (wz, wy, wx, wxl, k, seeds, owners, diag, u2, rhs_ref, first_ref, ints, u1, acc) = refs
    s = shape
    slab = lax.axis_index("slab")
    row = lax.axis_index("row")
    cy, oy, oz = s.cy, s.oy, s.oz
    strips, _ = s.strips()

    def sides(below_ref, above_ref):
        for z, at, count in strips:
            for a in range(5):
                ints[a, oz + z, oy - count : oy] = below_ref[a, at : at + count]
                ints[a, oz + z, oy + cy : oy + cy + count] = above_ref[a, at : at + count]

    @pl.when(row % 2 == 0)
    def _():
        sides(odd_ref, even_ref)

    @pl.when(row % 2 == 1)
    def _():
        sides(even_ref, odd_ref)

    def prepare(i, lower_wz):
        for a in range(5):
            ints[a, i, oy : oy + cy] = frame_ref[a, i]
        plane = slab * s.cz + i - oz
        line = row * cy - oy + lax.broadcasted_iota(jnp.int32, (s.rows, s.nx), 0)
        column = lax.broadcasted_iota(jnp.int32, (s.rows, s.nx), 1)
        keep_plane = jnp.logical_and(plane != -1, plane != s.cz * s.n_slab - 1)
        keep_line = jnp.logical_and(line != -1, line != cy * s.n_row - 1)
        w_z = ints[0, i].astype(jnp.float32) * jnp.where(keep_plane, weight_unit, 0.0)
        w_y = jnp.where(keep_line, ints[1, i].astype(jnp.float32) * weight_unit, 0.0)
        w_x = jnp.where(column < s.nx - 1, ints[2, i].astype(jnp.float32) * weight_unit, 0.0)
        w_xl = pltpu.roll(w_x, 1, axis=1)
        seed = ints[3, i]
        d = (
            prior_mass
            + seed_weight * (seed >= 0).astype(jnp.float32)
            + w_z
            + w_y
            + w_x
            + lower_wz
            + pltpu.roll(w_y, 1, axis=0)
            + w_xl
        )
        wz[i] = w_z
        wy[i] = w_y
        wx[i] = w_x
        wxl[i] = w_xl
        k[i] = smooth_step / d
        diag[i] = d
        seeds[i] = seed
        owners[i] = ints[4, i]
        return w_z

    lax.fori_loop(0, s.planes, prepare, jnp.zeros((s.rows, s.nx), jnp.float32))
    fields = Fields(s, wz, wy, wx, wxl, k, seeds)
    at1 = (NEED, NEED)

    def start(z, lo, hi):
        for y in range(lo, hi):
            kk = row_of(k, z + oz, y + oy, s.nx)
            seed = row_of(seeds, z + oz, y + oy, s.nx)
            u1[z + at1[0], y + at1[1]] = jnp.where(seed == fields.lab, seed_weight * kk, 0.0)

    fields.region(NEED, start)
    at2 = (NEED - 1, NEED - 1)
    fields.sweep(u1, at1, u2, at2, NEED - 1)
    rhs = fields.coarse_sums(u2, at2, diag, oz, owners, acc)
    rhs_ref[...] = rhs
    first = coarse_step * rhs / own_diagonal(blocks_ref, s)
    for t in range(s.group):
        first_ref[t] = first


def coarse_kernel(shape, first_ref, rhs_ref, blocks_ref, second_ref):
    s = shape
    turn = lax.axis_index("slab") // s.sections
    mine = first_ref[turn]
    whole = jnp.concatenate([first_ref[t] for t in range(s.group)], axis=1)
    applied = lax.dot_general(
        whole,
        blocks_ref[...],
        (((1,), (1,)), ((), ())),
        precision=lax.Precision.HIGHEST,
        preferred_element_type=jnp.float32,
    )
    second = mine + coarse_step * (rhs_ref[...] - applied) / own_diagonal(blocks_ref, s)
    for i in range(second_ref.shape[0]):
        second_ref[i] = second


def middle_kernel(shape, second_ref, blocks_ref, wz, wy, wx, wxl, k, seeds, owners, diag, u2, *refs):
    (u5, rhs_ref, first_ref, u3, u4, acc) = refs
    s = shape
    slab = lax.axis_index("slab")
    row = lax.axis_index("row")
    fields = Fields(s, wz, wy, wx, wxl, k, seeds)
    layers = NEED - 1
    at2 = (layers, layers)

    def table(dz, dy):
        i = jnp.clip(slab + dz, 0, s.n_slab - 1) * s.n_row + jnp.clip(row + dy, 0, s.n_row - 1)
        return second_ref[i]

    def correct(z, lo, hi):
        dz = lax.div(z + s.oz, s.cz) - s.reach
        for dy in (-1, 0, 1):
            begin, end = max(lo, dy * s.cy), min(hi, (dy + 1) * s.cy)
            if begin >= end:
                continue
            tab = table(dz, dy)
            for y in range(begin, end):
                ids = owners[z + s.oz, y + s.oy : y + s.oy + 1, :]
                at = (z + at2[0], y + at2[1])
                u4[at] = u2[at] + take(tab, ids, s)

    fields.region(layers, correct)
    fields.sweep(u4, at2, u3, at2, layers - 1)
    fields.sweep(u3, at2, u4, at2, layers - 2)
    fields.sweep(u4, at2, u5, (1, 1), 1)
    rhs = fields.coarse_sums(u5, (1, 1), diag, s.oz, owners, acc)
    rhs_ref[...] = rhs
    first = coarse_step * rhs / own_diagonal(blocks_ref, s)
    for t in range(s.group):
        first_ref[t] = first


def last_kernel(shape, own_ref, z0, z1, y0, y1, wz, wy, wx, wxl, k, seeds, owners, u5, out_ref, u6):
    s = shape
    slab = lax.axis_index("slab")
    row = lax.axis_index("row")
    fields = Fields(s, wz, wy, wx, wxl, k, seeds)

    def pick(even, first, second):
        return jnp.where(even, first[0], second[0])

    up_z = pick(slab % 2 == 0, z0, z1)
    down_z = pick(slab % 2 == 0, z1, z0)
    up_y = pick(row % 2 == 0, y0, y1)
    down_y = pick(row % 2 == 0, y1, y0)

    def add(z, y, tab):
        ids = owners[z + s.oz, y + s.oy : y + s.oy + 1, :]
        u6[z + 1, y + 1] = u5[z + 1, y + 1] + take(tab, ids, s)

    own = own_ref[0]
    for y in range(s.cy):
        add(-1, y, down_z)
        add(s.cz, y, up_z)

    def plane(z, c):
        add(z, -1, down_y)
        add(z, s.cy, up_y)
        for y in range(s.cy):
            add(z, y, own)
        return c

    lax.fori_loop(0, s.cz, plane, 0)

    def body(z, lo, hi):
        def use(y, centre, near):
            kk = row_of(k, z + s.oz, y + s.oy, s.nx)
            out_ref[:, z, y, :] = (1.0 - smooth_step) * centre + kk * (fields.source(z, y) + near)

        fields.near_rows(u6, 1, 1, z, lo, hi, use)

    fields.region(0, body)


def f32(*dims):
    return jax.ShapeDtypeStruct(dims, jnp.float32)


def i32(*dims):
    return jax.ShapeDtypeStruct(dims, jnp.int32)


def per_device(edge_weights, seeds, supervoxel, coarse_blocks):
    import functools

    s = Shape(edge_weights, coarse_blocks)
    blocks = coarse_blocks[0]
    own = jnp.concatenate([edge_weights, seeds[None], supervoxel[None]], axis=0)
    recvs = [swap(own, "slab", d, ph) for d in range(1, s.reach + 1) for ph in (0, 1)]
    _, packed = s.strips()
    frame, even, odd = pl.pallas_call(
        functools.partial(pack_kernel, s),
        out_shape=(i32(5, s.planes, s.cy, s.nx), i32(5, packed, s.nx), i32(5, packed, s.nx)),
        in_specs=vmem(1 + len(recvs)),
        out_specs=tuple(vmem(3)),
        compiler_params=params(),
        name="pack",
    )(own, *recvs)
    even = swap(even, "row", 1, 0)
    odd = swap(odd, "row", 1, 1)
    plane = (s.planes, s.rows, s.nx)
    wide = 2 * (NEED - 1)
    *kept, u2, rhs, first = pl.pallas_call(
        functools.partial(down_kernel, s),
        out_shape=tuple(
            [f32(*plane)] * 5
            + [i32(*plane)] * 2
            + [f32(*plane), f32(s.cz + wide, s.cy + wide, LABELS, s.nx)]
            + [f32(LABELS, s.cc), f32(s.group, LABELS, s.cc)]
        ),
        in_specs=vmem(4),
        out_specs=tuple(vmem(11)),
        scratch_shapes=[
            pltpu.VMEM((5,) + plane, jnp.int32),
            pltpu.VMEM((s.cz + 2 * NEED, s.cy + 2 * NEED, LABELS, s.nx), jnp.float32),
            pltpu.VMEM((3 * LABELS, s.cc), jnp.float32),
        ],
        compiler_params=params(),
        name="down",
    )(frame, even, odd, blocks)
    diag = kept[7]

    groups = [[t * s.sections + g for t in range(s.group)] for g in range(s.sections)]

    def coarse(first, rhs, copies):
        gathered = lax.all_to_all(
            first, "slab", 0, 0, axis_index_groups=groups if s.sections > 1 else None, tiled=True
        )
        return pl.pallas_call(
            functools.partial(coarse_kernel, s),
            out_shape=f32(copies, LABELS, s.cc),
            in_specs=vmem(3),
            out_specs=vmem(1)[0],
            compiler_params=params(),
            name="coarse",
        )(gathered, rhs, blocks)

    second = coarse(first, rhs, s.n_slab * s.n_row)
    second = lax.all_to_all(second, BOTH, 0, 0, tiled=True)
    u5, rhs, first = pl.pallas_call(
        functools.partial(middle_kernel, s),
        out_shape=(
            f32(s.cz + 2, s.cy + 2, LABELS, s.nx),
            f32(LABELS, s.cc),
            f32(s.group, LABELS, s.cc),
        ),
        in_specs=vmem(11),
        out_specs=tuple(vmem(3)),
        scratch_shapes=[
            pltpu.VMEM((s.cz + wide, s.cy + wide, LABELS, s.nx), jnp.float32),
            pltpu.VMEM((s.cz + wide, s.cy + wide, LABELS, s.nx), jnp.float32),
            pltpu.VMEM((3 * LABELS, s.cc), jnp.float32),
        ],
        compiler_params=params(),
        name="middle",
    )(second, blocks, *kept[:7], diag, u2)
    second = coarse(first, rhs, 1)
    around = [swap(second, axis, 1, ph) for axis in ("slab", "row") for ph in (0, 1)]
    return pl.pallas_call(
        functools.partial(last_kernel, s),
        out_shape=f32(LABELS, s.cz, s.cy, s.nx),
        in_specs=vmem(13),
        out_specs=vmem(1)[0],
        scratch_shapes=[pltpu.VMEM((s.cz + 2, s.cy + 2, LABELS, s.nx), jnp.float32)],
        compiler_params=params(),
        name="last",
    )(second, *around, *kept[:7], u5)


def solution(mesh):
    in_specs = (
        P(None, "slab", "row", None),
        P("slab", "row", None),
        P("slab", "row", None),
        P("row", "slab", None),
    )
    out_specs = P(None, "slab", "row", None)
    return jax.shard_map(
        per_device, mesh=mesh, in_specs=in_specs, out_specs=out_specs, check_vma=False
    )
```

```python
import functools

import jax
import jax.numpy as jnp
from jax import lax
from jax.experimental import pallas as pl
from jax.experimental.pallas import tpu as pltpu
from jax.sharding import PartitionSpec as P

LABELS = 8
ARRAYS = 5

prior_mass = 0.25
seed_weight = 4.0
smooth_step = 0.8
coarse_step = 0.7
weight_unit = 0.125

BOTH = ("slab", "row")
NEED = 5
VMEM_LIMIT = 24 * 1024 * 1024


def pairing(n_slab, n_row, axis, distance, phase):
    count = n_slab if axis == "slab" else n_row
    spare = n_row if axis == "slab" else n_slab
    pairs = []
    for s in range(n_slab):
        for r in range(n_row):
            i, other = (s, r) if axis == "slab" else (r, s)
            if (i // distance) % 2 == phase and i + distance < count:
                j, k = i + distance, other
            elif i >= distance and (i // distance - 1) % 2 == phase:
                j, k = i - distance, other
            elif spare % 2 == 0:
                j, k = i, other ^ 1
            else:
                continue
            target = (j, k) if axis == "slab" else (k, j)
            pairs.append((s * n_row + r, target[0] * n_row + target[1]))
    return pairs


def swap(block, axis, distance, phase):
    n_slab, n_row = lax.axis_size("slab"), lax.axis_size("row")
    return lax.ppermute(block, BOTH, pairing(n_slab, n_row, axis, distance, phase))


def vmem(count):
    return [pl.BlockSpec(memory_space=pltpu.VMEM)] * count


def params():
    return pltpu.CompilerParams(vmem_limit_bytes=VMEM_LIMIT)


class Shape:
    def __init__(self, edge_weights, coarse_blocks):
        self.cz, self.cy, self.nx = edge_weights.shape[1:]
        self.cc = coarse_blocks.shape[1]
        self.group = coarse_blocks.shape[2] // self.cc
        self.n_slab = lax.axis_size("slab")
        self.n_row = lax.axis_size("row")
        self.sections = self.n_slab // self.group
        self.reach = -(-(NEED + 1) // self.cz)
        self.oz = self.reach * self.cz
        self.planes = self.cz + 2 * self.oz
        self.rows = 3 * self.cy
        self.oy = self.cy
        full = ARRAYS * self.cz
        self.partial = [
            d for d in range(1, self.reach + 1) if min(map(len, self.plane_items(d))) < full
        ]

    def away(self, z):
        return -z if z < 0 else max(0, z - self.cz + 1)

    def needed(self, z):
        base = NEED - self.away(z)
        next_plane = 1 if z < 0 else 0
        below = (base + next_plane, base + 1, base, base, base - 1)
        above = (base + next_plane, base, base, base, base - 1)
        return [(max(-1, lo), max(-1, hi)) for lo, hi in zip(below, above)]

    def plane_items(self, distance):
        items = [(a, z) for a in range(ARRAYS) for z in range(self.cz)]
        shift = distance * self.cz
        up = [(a, z) for a, z in items if self.wanted(a, z - shift) >= 0]
        down = [(a, z) for a, z in items if self.wanted(a, z + shift) >= 0]
        return up, down

    def wanted(self, a, z):
        base = NEED - self.away(z)
        return (base + (1 if z < 0 else 0), base, base, base, base - 1)[a]

    def row_items(self, side):
        out, at = [], 0
        for z in range(-self.oz, self.cz + self.oz):
            for a, counts in enumerate(self.needed(z)):
                if counts[side] > 0:
                    out.append((a, z, at, counts[side]))
                    at += counts[side]
        return out, at


def parity_of(index, distance):
    return (index // distance) % 2


def start_kernel(shape, edge_ref, seeds_ref, owners_ref, blocks_in, own_ref, blocks_ref, *refs):
    sems = refs[-1]
    cz = shape.cz
    copies = [
        pltpu.make_async_copy(source, own_ref.at[pl.ds(a * cz, cz)], sems.at[a])
        for a, source in enumerate([edge_ref.at[0], edge_ref.at[1], edge_ref.at[2], seeds_ref, owners_ref])
    ]
    fetch = pltpu.make_async_copy(blocks_in, blocks_ref, sems.at[ARRAYS])
    for copy in copies:
        copy.start()
    fetch.start()
    for copy in copies:
        copy.wait()
    slab = lax.axis_index("slab")
    for i, d in enumerate(shape.partial):
        first_ref, second_ref = refs[2 * i], refs[2 * i + 1]
        up, down = shape.plane_items(d)

        def fill(up_ref, down_ref, up=up, down=down):
            for items, ref in ((up, up_ref), (down, down_ref)):
                for n in range(ref.shape[0]):
                    a, z = items[min(n, len(items) - 1)]
                    ref[n] = own_ref[a * cz + z]

        @pl.when(parity_of(slab, d) == 0)
        def _():
            fill(first_ref, second_ref)

        @pl.when(parity_of(slab, d) == 1)
        def _():
            fill(second_ref, first_ref)

    fetch.wait()


def pack_kernel(shape, own_ref, blocks_ref, *refs):
    recvs, (frame_ref, even_ref, odd_ref, dc_ref) = refs[:-4], refs[-4:]
    cz, oz = shape.cz, shape.oz
    slab = lax.axis_index("slab")
    row = lax.axis_index("row")
    for a in range(ARRAYS):
        for z in range(cz):
            frame_ref[a, oz + z] = own_ref[a * cz + z]
    for d in range(1, shape.reach + 1):
        first, second = recvs[2 * d - 2], recvs[2 * d - 1]
        up, down = shape.plane_items(d)

        def place(above, below, d=d, up=up, down=down):
            for n, (a, z) in enumerate(down):
                frame_ref[a, oz + d * cz + z] = above[n]
            for n, (a, z) in enumerate(up):
                frame_ref[a, oz - d * cz + z] = below[n]

        @pl.when(parity_of(slab, d) == 0)
        def _():
            place(first, second)

        @pl.when(parity_of(slab, d) == 1)
        def _():
            place(second, first)

    def fill(last_ref, first_ref):
        for a, z, at, count in shape.row_items(0)[0]:
            last_ref[at : at + count] = frame_ref[a, oz + z, shape.cy - count :]
        for a, z, at, count in shape.row_items(1)[0]:
            first_ref[at : at + count] = frame_ref[a, oz + z, :count]

    @pl.when(row % 2 == 0)
    def _():
        fill(even_ref, odd_ref)

    @pl.when(row % 2 == 1)
    def _():
        fill(odd_ref, even_ref)

    turn = slab // shape.sections
    block = blocks_ref[:, pl.ds(pl.multiple_of(turn * shape.cc, shape.cc), shape.cc)]
    a = lax.broadcasted_iota(jnp.int32, block.shape, 0)
    b = lax.broadcasted_iota(jnp.int32, block.shape, 1)
    dc_ref[...] = jnp.sum(jnp.where(a == b, block, 0.0), axis=0, keepdims=True)


def row_of(ref, z, y, count):
    return jnp.broadcast_to(ref[z, y : y + 1, :], (LABELS, count))


class Fields:
    def __init__(self, shape, faces, u1):
        self.s, self.faces, self.u1 = shape, faces, u1

    def region(self, layers, body):
        s = self.s
        for m in range(layers + 1):
            lo, hi = -(layers - m), s.cy + layers - m

            def inner(i, c, m=m, lo=lo, hi=hi):
                body(i if m == 0 else jnp.where(i == 0, -m, s.cz - 1 + m), lo, hi)
                return c

            lax.fori_loop(0, s.cz if m == 0 else 2, inner, 0)

    def moved_rows(self, src, at, z, lo, hi, use):
        s = self.s
        zz, z, z1 = z + s.oz, z + at, z + NEED
        before = src[z, lo - 1 + at]
        centre = src[z, lo + at]
        for y in range(lo, hi):
            above_z, below_z, above_y, below_y, above_x, below_x = [
                row_of(face, zz, y + s.oy, s.nx) for face in self.faces
            ]
            after = src[z, y + 1 + at]
            total = above_x * pltpu.roll(centre, s.nx - 1, axis=1)
            total += below_x * pltpu.roll(centre, 1, axis=1)
            total += above_y * after + below_y * before
            total += above_z * src[z + 1, y + at] + below_z * src[z - 1, y + at]
            use(y, centre, total + self.u1[z1, y + NEED])
            before, centre = centre, after

    def sweep(self, src, src_at, dst, dst_at, layers):
        def body(z, lo, hi):
            def use(y, centre, total):
                dst[z + dst_at, y + dst_at] = (1.0 - smooth_step) * centre + total

            self.moved_rows(src, src_at, z, lo, hi, use)

        self.region(layers, body)

    def coarse_sums(self, src, src_at, scale, owners, acc):
        s = self.s
        acc[...] = jnp.zeros_like(acc)
        cells = lax.broadcasted_iota(jnp.int32, (s.cc, s.nx), 0)

        def body(z, lo, hi):
            def use(y, centre, total):
                rest = row_of(scale, z, y + s.oy, s.nx) * (total - smooth_step * centre)
                top = rest.astype(jnp.bfloat16).astype(jnp.float32)
                mid = (rest - top).astype(jnp.bfloat16).astype(jnp.float32)
                low = rest - top - mid
                parts = jnp.concatenate([top, mid, low], axis=0).astype(jnp.bfloat16)
                ids = jnp.broadcast_to(owners[z + s.oz, y + s.oy : y + s.oy + 1, :], (s.cc, s.nx))
                onehot = jnp.where(ids == cells, 1.0, 0.0).astype(jnp.bfloat16)
                acc[...] += lax.dot_general(
                    parts, onehot, (((1,), (1,)), ((), ())), preferred_element_type=jnp.float32
                )

            self.moved_rows(src, src_at, z, lo, hi, use)

        self.region(0, body)
        return acc[0:LABELS] + acc[LABELS : 2 * LABELS] + acc[2 * LABELS : 3 * LABELS]


def take(table, ids, shape):
    ids = jnp.broadcast_to(ids, (LABELS, shape.nx))
    numbers = lax.GatherDimensionNumbers(
        offset_dims=(),
        collapsed_slice_dims=(1,),
        start_index_map=(1,),
        operand_batching_dims=(0,),
        start_indices_batching_dims=(0,),
    )
    parts = [
        lax.gather(
            table,
            ids[:, i : i + shape.cc, None],
            numbers,
            (1, 1),
            mode=lax.GatherScatterMode.PROMISE_IN_BOUNDS,
        )
        for i in range(0, shape.nx, shape.cc)
    ]
    return jnp.concatenate(parts, axis=1)


def down_kernel(shape, frame_ref, even_ref, odd_ref, dc_ref, *refs):
    faces, (u1, owners, scale, u2, rhs_ref, first_ref, kept, ints, acc) = refs[:6], refs[6:]
    s = shape
    slab = lax.axis_index("slab")
    row = lax.axis_index("row")
    cz, cy, oy, oz = s.cz, s.cy, s.oy, s.oz

    def sides(below_ref, above_ref):
        for a, z, at, count in s.row_items(0)[0]:
            ints[a, oz + z, oy - count : oy] = below_ref[at : at + count]
        for a, z, at, count in s.row_items(1)[0]:
            ints[a, oz + z, oy + cy : oy + cy + count] = above_ref[at : at + count]

    @pl.when(row % 2 == 0)
    def _():
        sides(odd_ref, even_ref)

    @pl.when(row % 2 == 1)
    def _():
        sides(even_ref, odd_ref)

    labels = lax.broadcasted_iota(jnp.int32, (LABELS, s.nx), 0)
    line = row * cy - oy + lax.broadcasted_iota(jnp.int32, (s.rows, s.nx), 0)
    column = lax.broadcasted_iota(jnp.int32, (s.rows, s.nx), 1)
    inside_y = jnp.logical_and(line >= 0, line < cy * s.n_row)
    unit_y = jnp.where(jnp.logical_and(line != -1, line != cy * s.n_row - 1), weight_unit, 0.0)
    unit_x = jnp.where(column < s.nx - 1, weight_unit, 0.0)

    def weights_z(i):
        plane = slab * cz + i - oz
        inside = jnp.logical_and(plane != -1, plane != cz * s.n_slab - 1)
        return ints[0, i].astype(jnp.float32) * jnp.where(inside, weight_unit, 0.0)

    def prepare(i, below_z):
        for a in range(ARRAYS):
            ints[a, i, oy : oy + cy] = frame_ref[a, i]
        w_z = weights_z(i)
        w_y = ints[1, i].astype(jnp.float32) * unit_y
        w_x = ints[2, i].astype(jnp.float32) * unit_x
        below_y = pltpu.roll(w_y, 1, axis=0)
        below_x = pltpu.roll(w_x, 1, axis=1)
        seeded = jnp.where(ints[3, i] >= 0, seed_weight + prior_mass, prior_mass)
        d = seeded + w_z + w_y + w_x + below_z + below_y + below_x
        plane = slab * cz + i - oz
        inside_z = jnp.logical_and(plane >= 0, plane < cz * s.n_slab)
        inside = jnp.logical_and(inside_y, inside_z)
        k = jnp.where(inside, smooth_step / d, 0.0)
        for face, w in zip(faces, (w_z, below_z, w_y, below_y, w_x, below_x)):
            face[i] = k * w
        kept[i] = seed_weight * k
        owners[i] = jnp.where(inside, ints[4, i], 0)

        @pl.when(jnp.logical_and(i >= oz, i < oz + cz))
        def _():
            scale[jnp.clip(i - oz, 0, cz - 1)] = d / smooth_step

        return w_z

    ints[0, 0, oy : oy + cy] = frame_ref[0, 0]
    lax.fori_loop(1, s.planes - 1, prepare, weights_z(0))
    fields = Fields(s, faces, u1)

    def start(z, lo, hi):
        for y in range(lo, hi):
            seed = jnp.broadcast_to(ints[3, z + oz, y + oy : y + oy + 1, :], (LABELS, s.nx))
            value = row_of(kept, z + oz, y + oy, s.nx)
            u1[z + NEED, y + NEED] = jnp.where(seed == labels, value, 0.0)

    fields.region(NEED, start)
    fields.sweep(u1, NEED, u2, NEED - 1, NEED - 1)
    rhs = fields.coarse_sums(u2, NEED - 1, scale, owners, acc)
    rhs_ref[...] = rhs
    first = coarse_step * rhs / dc_ref[...]
    for t in range(s.group):
        first_ref[t] = first


def coarse_kernel(shape, first_ref, rhs_ref, blocks_ref, dc_ref, second_ref):
    s = shape
    turn = lax.axis_index("slab") // s.sections
    mine = first_ref[turn]
    whole = jnp.concatenate([first_ref[t] for t in range(s.group)], axis=1)
    applied = lax.dot_general(
        whole,
        blocks_ref[...],
        (((1,), (1,)), ((), ())),
        precision=lax.Precision.HIGHEST,
        preferred_element_type=jnp.float32,
    )
    second = mine + coarse_step * (rhs_ref[...] - applied) / dc_ref[...]
    for i in range(second_ref.shape[0]):
        second_ref[i] = second


def middle_kernel(shape, second_ref, dc_ref, *refs):
    faces, (u1, owners, scale, u2, u5, rhs_ref, first_ref, u3, u4, acc) = refs[:6], refs[6:]
    s = shape
    slab = lax.axis_index("slab")
    row = lax.axis_index("row")
    fields = Fields(s, faces, u1)
    layers = NEED - 1

    def table(dz, dy):
        i = jnp.clip(slab + dz, 0, s.n_slab - 1) * s.n_row + jnp.clip(row + dy, 0, s.n_row - 1)
        return second_ref[i]

    def correct(z, lo, hi):
        dz = lax.div(z + s.oz, s.cz) - s.reach
        for dy in (-1, 0, 1):
            begin, end = max(lo, dy * s.cy), min(hi, (dy + 1) * s.cy)
            if begin >= end:
                continue
            tab = table(dz, dy)
            for y in range(begin, end):
                ids = owners[z + s.oz, y + s.oy : y + s.oy + 1, :]
                at = (z + layers, y + layers)
                u4[at] = u2[at] + take(tab, ids, s)

    fields.region(layers, correct)
    fields.sweep(u4, layers, u3, layers, layers - 1)
    fields.sweep(u3, layers, u4, layers, layers - 2)
    fields.sweep(u4, layers, u5, 1, 1)
    rhs = fields.coarse_sums(u5, 1, scale, owners, acc)
    rhs_ref[...] = rhs
    first = coarse_step * rhs / dc_ref[...]
    for t in range(s.group):
        first_ref[t] = first


def last_kernel(shape, own_ref, z0, z1, y0, y1, *refs):
    faces, (u1, owners, u5, out_ref, u6) = refs[:6], refs[6:]
    s = shape
    slab = lax.axis_index("slab")
    row = lax.axis_index("row")
    fields = Fields(s, faces, u1)

    def pick(even, first, second):
        return jnp.where(even, first[0], second[0])

    up_z = pick(slab % 2 == 0, z0, z1)
    down_z = pick(slab % 2 == 0, z1, z0)
    up_y = pick(row % 2 == 0, y0, y1)
    down_y = pick(row % 2 == 0, y1, y0)

    def add(z, y, tab):
        ids = owners[z + s.oz, y + s.oy : y + s.oy + 1, :]
        u6[z + 1, y + 1] = u5[z + 1, y + 1] + take(tab, ids, s)

    own = own_ref[0]
    for y in range(s.cy):
        add(-1, y, down_z)
        add(s.cz, y, up_z)

    def plane(z, c):
        add(z, -1, down_y)
        add(z, s.cy, up_y)
        for y in range(s.cy):
            add(z, y, own)
        return c

    lax.fori_loop(0, s.cz, plane, 0)

    def body(z, lo, hi):
        def use(y, centre, total):
            out_ref[:, z, y, :] = (1.0 - smooth_step) * centre + total

        fields.moved_rows(u6, 1, z, lo, hi, use)

    fields.region(0, body)


def f32(*dims):
    return jax.ShapeDtypeStruct(dims, jnp.float32)


def i32(*dims):
    return jax.ShapeDtypeStruct(dims, jnp.int32)


def per_device(edge_weights, seeds, supervoxel, coarse_blocks):
    s = Shape(edge_weights, coarse_blocks)
    messages = []
    for d in s.partial:
        count = max(len(items) for items in s.plane_items(d))
        messages += [i32(count, s.cy, s.nx)] * 2
    own, blocks, *messages = pl.pallas_call(
        functools.partial(start_kernel, s),
        out_shape=tuple(
            [i32(ARRAYS * s.cz, s.cy, s.nx), f32(*coarse_blocks.shape[1:])] + messages
        ),
        in_specs=[pl.BlockSpec(memory_space=pltpu.HBM)] * 4,
        out_specs=tuple(vmem(2 + len(messages))),
        scratch_shapes=[pltpu.SemaphoreType.DMA((ARRAYS + 1,))],
        compiler_params=params(),
        name="start",
    )(*[pltpu.with_memory_space_constraint(x, pltpu.HBM) for x in (edge_weights, seeds, supervoxel, coarse_blocks[0])])
    recvs = []
    for d in range(1, s.reach + 1):
        for ph in (0, 1):
            sent = messages[2 * s.partial.index(d) + ph] if d in s.partial else own
            recvs.append(swap(sent, "slab", d, ph))
    rows = -(-max(s.row_items(0)[1], s.row_items(1)[1]) // 8) * 8
    frame, even, odd, dc = pl.pallas_call(
        functools.partial(pack_kernel, s),
        out_shape=(
            i32(ARRAYS, s.planes, s.cy, s.nx),
            i32(rows, s.nx),
            i32(rows, s.nx),
            f32(1, s.cc),
        ),
        in_specs=vmem(2 + len(recvs)),
        out_specs=tuple(vmem(4)),
        compiler_params=params(),
        name="pack",
    )(own, blocks, *recvs)
    even = swap(even, "row", 1, 0)
    odd = swap(odd, "row", 1, 1)
    plane = (s.planes, s.rows, s.nx)
    wide = 2 * (NEED - 1)
    *faces, u1, owners, scale, u2, rhs, first = pl.pallas_call(
        functools.partial(down_kernel, s),
        out_shape=tuple(
            [f32(*plane)] * 6
            + [f32(s.cz + 2 * NEED, s.cy + 2 * NEED, LABELS, s.nx), i32(*plane)]
            + [f32(s.cz, s.rows, s.nx), f32(s.cz + wide, s.cy + wide, LABELS, s.nx)]
            + [f32(LABELS, s.cc), f32(s.group, LABELS, s.cc)]
        ),
        in_specs=vmem(4),
        out_specs=tuple(vmem(12)),
        scratch_shapes=[
            pltpu.VMEM(plane, jnp.float32),
            pltpu.VMEM((ARRAYS,) + plane, jnp.int32),
            pltpu.VMEM((3 * LABELS, s.cc), jnp.float32),
        ],
        compiler_params=params(),
        name="down",
    )(frame, even, odd, dc)

    groups = [[t * s.sections + g for t in range(s.group)] for g in range(s.sections)]

    def coarse(first, rhs, copies):
        gathered = lax.all_to_all(
            first, "slab", 0, 0, axis_index_groups=groups if s.sections > 1 else None, tiled=True
        )
        return pl.pallas_call(
            functools.partial(coarse_kernel, s),
            out_shape=f32(copies, LABELS, s.cc),
            in_specs=vmem(4),
            out_specs=vmem(1)[0],
            compiler_params=params(),
            name="coarse",
        )(gathered, rhs, blocks, dc)

    second = coarse(first, rhs, s.n_slab * s.n_row)
    second = lax.all_to_all(second, BOTH, 0, 0, tiled=True)
    u5, rhs, first = pl.pallas_call(
        functools.partial(middle_kernel, s),
        out_shape=(
            f32(s.cz + 2, s.cy + 2, LABELS, s.nx),
            f32(LABELS, s.cc),
            f32(s.group, LABELS, s.cc),
        ),
        in_specs=vmem(12),
        out_specs=tuple(vmem(3)),
        scratch_shapes=[
            pltpu.VMEM((s.cz + wide, s.cy + wide, LABELS, s.nx), jnp.float32),
            pltpu.VMEM((s.cz + wide, s.cy + wide, LABELS, s.nx), jnp.float32),
            pltpu.VMEM((3 * LABELS, s.cc), jnp.float32),
        ],
        compiler_params=params(),
        name="middle",
    )(second, dc, *faces, u1, owners, scale, u2)
    second = coarse(first, rhs, 1)
    around = [swap(second, axis, 1, ph) for axis in ("slab", "row") for ph in (0, 1)]
    return pl.pallas_call(
        functools.partial(last_kernel, s),
        out_shape=f32(LABELS, s.cz, s.cy, s.nx),
        in_specs=vmem(14),
        out_specs=vmem(1)[0],
        scratch_shapes=[pltpu.VMEM((s.cz + 2, s.cy + 2, LABELS, s.nx), jnp.float32)],
        compiler_params=params(),
        name="last",
    )(second, *around, *faces, u1, owners, u5)


def solution(mesh):
    in_specs = (
        P(None, "slab", "row", None),
        P("slab", "row", None),
        P("slab", "row", None),
        P("row", "slab", None),
    )
    out_specs = P(None, "slab", "row", None)
    return jax.shard_map(
        per_device, mesh=mesh, in_specs=in_specs, out_specs=out_specs, check_vma=False
    )
```

```python
import functools

import jax
import jax.numpy as jnp
from jax import lax
from jax.experimental import pallas as pl
from jax.experimental.pallas import tpu as pltpu
from jax.sharding import PartitionSpec as P

LABELS = 8
ARRAYS = 5

prior_mass = 0.25
seed_weight = 4.0
smooth_step = 0.8
coarse_step = 0.7
weight_unit = 0.125

BOTH = ("slab", "row")
NEED = 5
VMEM_LIMIT = 24 * 1024 * 1024


def pairing(n_slab, n_row, axis, distance, phase):
    count = n_slab if axis == "slab" else n_row
    spare = n_row if axis == "slab" else n_slab
    pairs = []
    for s in range(n_slab):
        for r in range(n_row):
            i, other = (s, r) if axis == "slab" else (r, s)
            if (i // distance) % 2 == phase and i + distance < count:
                j, k = i + distance, other
            elif i >= distance and (i // distance - 1) % 2 == phase:
                j, k = i - distance, other
            elif spare % 2 == 0:
                j, k = i, other ^ 1
            else:
                continue
            target = (j, k) if axis == "slab" else (k, j)
            pairs.append((s * n_row + r, target[0] * n_row + target[1]))
    return pairs


def swap(block, axis, distance, phase):
    n_slab, n_row = lax.axis_size("slab"), lax.axis_size("row")
    return lax.ppermute(block, BOTH, pairing(n_slab, n_row, axis, distance, phase))


def vmem(count):
    return [pl.BlockSpec(memory_space=pltpu.VMEM)] * count


def params():
    return pltpu.CompilerParams(vmem_limit_bytes=VMEM_LIMIT)


class Shape:
    def __init__(self, edge_weights, coarse_blocks):
        self.cz, self.cy, self.nx = edge_weights.shape[1:]
        self.cc = coarse_blocks.shape[1]
        self.group = coarse_blocks.shape[2] // self.cc
        self.n_slab = lax.axis_size("slab")
        self.n_row = lax.axis_size("row")
        self.sections = self.n_slab // self.group
        self.reach = -(-(NEED + 1) // self.cz)
        self.oz = self.reach * self.cz
        self.planes = self.cz + 2 * self.oz
        self.rows = 3 * self.cy
        self.oy = self.cy
        full = ARRAYS * self.cz
        self.partial = [
            d for d in range(1, self.reach + 1) if min(map(len, self.plane_items(d))) < full
        ]

    def away(self, z):
        return -z if z < 0 else max(0, z - self.cz + 1)

    def needed(self, z):
        base = NEED - self.away(z)
        next_plane = 1 if z < 0 else 0
        below = (base + next_plane, base + 1, base, base, base - 1)
        above = (base + next_plane, base, base, base, base - 1)
        return [(max(-1, lo), max(-1, hi)) for lo, hi in zip(below, above)]

    def plane_items(self, distance):
        items = [(a, z) for a in range(ARRAYS) for z in range(self.cz)]
        shift = distance * self.cz
        up = [(a, z) for a, z in items if self.wanted(a, z - shift) >= 0]
        down = [(a, z) for a, z in items if self.wanted(a, z + shift) >= 0]
        return up, down

    def wanted(self, a, z):
        base = NEED - self.away(z)
        return (base + (1 if z < 0 else 0), base, base, base, base - 1)[a]

    def row_items(self, side):
        out, at = [], 0
        for z in range(-self.oz, self.cz + self.oz):
            for a, counts in enumerate(self.needed(z)):
                if counts[side] > 0:
                    out.append((a, z, at, counts[side]))
                    at += counts[side]
        return out, at


def parity_of(index, distance):
    return (index // distance) % 2


def start_kernel(shape, edge_ref, seeds_ref, owners_ref, blocks_in, own_ref, blocks_ref, *refs):
    sems = refs[-1]
    cz = shape.cz
    copies = [
        pltpu.make_async_copy(source, own_ref.at[pl.ds(a * cz, cz)], sems.at[a])
        for a, source in enumerate([edge_ref.at[0], edge_ref.at[1], edge_ref.at[2], seeds_ref, owners_ref])
    ]
    fetch = pltpu.make_async_copy(blocks_in, blocks_ref, sems.at[ARRAYS])
    for copy in copies:
        copy.start()
    fetch.start()
    for copy in copies:
        copy.wait()
    slab = lax.axis_index("slab")
    for i, d in enumerate(shape.partial):
        first_ref, second_ref = refs[2 * i], refs[2 * i + 1]
        up, down = shape.plane_items(d)

        def fill(up_ref, down_ref, up=up, down=down):
            for items, ref in ((up, up_ref), (down, down_ref)):
                for n in range(ref.shape[0]):
                    a, z = items[min(n, len(items) - 1)]
                    ref[n] = own_ref[a * cz + z]

        @pl.when(parity_of(slab, d) == 0)
        def _():
            fill(first_ref, second_ref)

        @pl.when(parity_of(slab, d) == 1)
        def _():
            fill(second_ref, first_ref)

    fetch.wait()


def pack_kernel(shape, own_ref, blocks_ref, *refs):
    recvs, (frame_ref, even_ref, odd_ref, dc_ref) = refs[:-4], refs[-4:]
    cz, oz = shape.cz, shape.oz
    slab = lax.axis_index("slab")
    row = lax.axis_index("row")
    for a in range(ARRAYS):
        for z in range(cz):
            frame_ref[a, oz + z] = own_ref[a * cz + z]
    for d in range(1, shape.reach + 1):
        first, second = recvs[2 * d - 2], recvs[2 * d - 1]
        up, down = shape.plane_items(d)

        def place(above, below, d=d, up=up, down=down):
            for n, (a, z) in enumerate(down):
                frame_ref[a, oz + d * cz + z] = above[n]
            for n, (a, z) in enumerate(up):
                frame_ref[a, oz - d * cz + z] = below[n]

        @pl.when(parity_of(slab, d) == 0)
        def _():
            place(first, second)

        @pl.when(parity_of(slab, d) == 1)
        def _():
            place(second, first)

    def fill(last_ref, first_ref):
        for a, z, at, count in shape.row_items(0)[0]:
            last_ref[at : at + count] = frame_ref[a, oz + z, shape.cy - count :]
        for a, z, at, count in shape.row_items(1)[0]:
            first_ref[at : at + count] = frame_ref[a, oz + z, :count]

    @pl.when(row % 2 == 0)
    def _():
        fill(even_ref, odd_ref)

    @pl.when(row % 2 == 1)
    def _():
        fill(odd_ref, even_ref)

    turn = slab // shape.sections
    block = blocks_ref[:, pl.ds(pl.multiple_of(turn * shape.cc, shape.cc), shape.cc)]
    a = lax.broadcasted_iota(jnp.int32, block.shape, 0)
    b = lax.broadcasted_iota(jnp.int32, block.shape, 1)
    dc_ref[...] = jnp.sum(jnp.where(a == b, block, 0.0), axis=0, keepdims=True)


def row_of(ref, z, y, count):
    return jnp.broadcast_to(ref[z, y : y + 1, :], (LABELS, count))


class Fields:
    def __init__(self, shape, faces, u1):
        self.s, self.faces, self.u1 = shape, faces, u1

    def region(self, layers, body):
        s = self.s
        for z in range(-layers, s.cz + layers):
            reach = layers - s.away(z)
            body(z, -reach, s.cy + reach)

    def moved_rows(self, src, at, z, lo, hi, use):
        s = self.s
        zz, z, z1 = z + s.oz, z + at, z + NEED
        before = src[z, lo - 1 + at]
        centre = src[z, lo + at]
        for y in range(lo, hi):
            above_z, below_z, above_y, below_y, above_x, below_x = [
                row_of(face, zz, y + s.oy, s.nx) for face in self.faces
            ]
            after = src[z, y + 1 + at]
            total = above_x * pltpu.roll(centre, s.nx - 1, axis=1)
            total += below_x * pltpu.roll(centre, 1, axis=1)
            total += above_y * after + below_y * before
            total += above_z * src[z + 1, y + at] + below_z * src[z - 1, y + at]
            use(y, centre, total + self.u1[z1, y + NEED])
            before, centre = centre, after

    def sweep(self, src, src_at, dst, dst_at, layers):
        def body(z, lo, hi):
            def use(y, centre, total):
                dst[z + dst_at, y + dst_at] = (1.0 - smooth_step) * centre + total

            self.moved_rows(src, src_at, z, lo, hi, use)

        self.region(layers, body)

    def coarse_sums(self, src, src_at, scale, owners, acc):
        s = self.s
        acc[...] = jnp.zeros_like(acc)
        pack = 16
        cells = lax.broadcasted_iota(jnp.int32, (s.cc, s.nx), 0).astype(jnp.float32)
        cells = cells.astype(jnp.bfloat16).reshape(s.cc // pack, pack, s.nx)
        one, none = jnp.bfloat16(1), jnp.bfloat16(0)

        def body(z, lo, hi):
            def use(y, centre, total):
                rest = row_of(scale, z, y + s.oy, s.nx) * (total - smooth_step * centre)
                top = rest.astype(jnp.bfloat16).astype(jnp.float32)
                mid = (rest - top).astype(jnp.bfloat16).astype(jnp.float32)
                low = rest - top - mid
                parts = jnp.concatenate([top, mid, low], axis=0).astype(jnp.bfloat16)
                ids = owners[z + s.oz, y + s.oy : y + s.oy + 1, :].astype(jnp.float32)
                ids = jnp.broadcast_to(ids, (pack, s.nx)).astype(jnp.bfloat16)
                onehot = jnp.where(ids[None] == cells, one, none).reshape(s.cc, s.nx)
                acc[...] += lax.dot_general(
                    parts, onehot, (((1,), (1,)), ((), ())), preferred_element_type=jnp.float32
                )

            self.moved_rows(src, src_at, z, lo, hi, use)

        self.region(0, body)
        return acc[0:LABELS] + acc[LABELS : 2 * LABELS] + acc[2 * LABELS : 3 * LABELS]


def take(table, ids, shape):
    ids = jnp.broadcast_to(ids, (LABELS, shape.nx))
    numbers = lax.GatherDimensionNumbers(
        offset_dims=(),
        collapsed_slice_dims=(1,),
        start_index_map=(1,),
        operand_batching_dims=(0,),
        start_indices_batching_dims=(0,),
    )
    parts = [
        lax.gather(
            table,
            ids[:, i : i + shape.cc, None],
            numbers,
            (1, 1),
            mode=lax.GatherScatterMode.PROMISE_IN_BOUNDS,
        )
        for i in range(0, shape.nx, shape.cc)
    ]
    return jnp.concatenate(parts, axis=1)


def spread(tables, index, ids, dst, z, y):
    numbers = lax.GatherDimensionNumbers(
        offset_dims=(),
        collapsed_slice_dims=(1,),
        start_index_map=(1,),
        operand_batching_dims=(0,),
        start_indices_batching_dims=(0,),
    )
    count, width = ids.shape
    lanes = tables.shape[2]
    for x in range(0, width, lanes):
        part = ids[:, x : x + lanes, None]
        for l in range(LABELS):
            row = jnp.broadcast_to(tables[index, l : l + 1, :], (count, lanes))
            dst[z, y : y + count, l, x : x + lanes] = lax.gather(
                row, part, numbers, (1, 1), mode=lax.GatherScatterMode.PROMISE_IN_BOUNDS
            )


def down_kernel(shape, frame_ref, even_ref, odd_ref, dc_ref, *refs):
    faces, (u1, owners, scale, u2, rhs_ref, first_ref, kept, ints, acc) = refs[:6], refs[6:]
    s = shape
    slab = lax.axis_index("slab")
    row = lax.axis_index("row")
    cz, cy, oy, oz = s.cz, s.cy, s.oy, s.oz

    def sides(below_ref, above_ref):
        for a, z, at, count in s.row_items(0)[0]:
            ints[a, oz + z, oy - count : oy] = below_ref[at : at + count]
        for a, z, at, count in s.row_items(1)[0]:
            ints[a, oz + z, oy + cy : oy + cy + count] = above_ref[at : at + count]

    @pl.when(row % 2 == 0)
    def _():
        sides(odd_ref, even_ref)

    @pl.when(row % 2 == 1)
    def _():
        sides(even_ref, odd_ref)

    labels = lax.broadcasted_iota(jnp.int32, (LABELS, s.nx), 0)
    line = row * cy - oy + lax.broadcasted_iota(jnp.int32, (s.rows, s.nx), 0)
    column = lax.broadcasted_iota(jnp.int32, (s.rows, s.nx), 1)
    inside_y = jnp.logical_and(line >= 0, line < cy * s.n_row)
    unit_y = jnp.where(jnp.logical_and(line != -1, line != cy * s.n_row - 1), weight_unit, 0.0)
    unit_x = jnp.where(column < s.nx - 1, weight_unit, 0.0)

    def weights_z(i):
        plane = slab * cz + i - oz
        inside = jnp.logical_and(plane != -1, plane != cz * s.n_slab - 1)
        return ints[0, i].astype(jnp.float32) * jnp.where(inside, weight_unit, 0.0)

    def prepare(i, below_z):
        for a in range(ARRAYS):
            ints[a, i, oy : oy + cy] = frame_ref[a, i]
        w_z = weights_z(i)
        w_y = ints[1, i].astype(jnp.float32) * unit_y
        w_x = ints[2, i].astype(jnp.float32) * unit_x
        below_y = pltpu.roll(w_y, 1, axis=0)
        below_x = pltpu.roll(w_x, 1, axis=1)
        seeded = jnp.where(ints[3, i] >= 0, seed_weight + prior_mass, prior_mass)
        d = seeded + w_z + w_y + w_x + below_z + below_y + below_x
        plane = slab * cz + i - oz
        inside_z = jnp.logical_and(plane >= 0, plane < cz * s.n_slab)
        inside = jnp.logical_and(inside_y, inside_z)
        k = jnp.where(inside, smooth_step / d, 0.0)
        for face, w in zip(faces, (w_z, below_z, w_y, below_y, w_x, below_x)):
            face[i] = k * w
        kept[i] = seed_weight * k
        owners[i] = jnp.where(inside, ints[4, i], 0)

        @pl.when(jnp.logical_and(i >= oz, i < oz + cz))
        def _():
            scale[jnp.clip(i - oz, 0, cz - 1)] = d / smooth_step

        return w_z

    ints[0, 0, oy : oy + cy] = frame_ref[0, 0]
    lax.fori_loop(1, s.planes - 1, prepare, weights_z(0))
    fields = Fields(s, faces, u1)

    def start(z, lo, hi):
        for y in range(lo, hi):
            seed = jnp.broadcast_to(ints[3, z + oz, y + oy : y + oy + 1, :], (LABELS, s.nx))
            value = row_of(kept, z + oz, y + oy, s.nx)
            u1[z + NEED, y + NEED] = jnp.where(seed == labels, value, 0.0)

    fields.region(NEED, start)
    fields.sweep(u1, NEED, u2, NEED - 1, NEED - 1)
    rhs = fields.coarse_sums(u2, NEED - 1, scale, owners, acc)
    rhs_ref[...] = rhs
    first = coarse_step * rhs / dc_ref[...]
    for t in range(s.group):
        first_ref[t] = first


def coarse_kernel(shape, first_ref, rhs_ref, blocks_ref, dc_ref, second_ref):
    s = shape
    turn = lax.axis_index("slab") // s.sections
    mine = first_ref[turn]
    whole = jnp.concatenate([first_ref[t] for t in range(s.group)], axis=1)
    applied = lax.dot_general(
        whole,
        blocks_ref[...],
        (((1,), (1,)), ((), ())),
        precision=lax.Precision.HIGHEST,
        preferred_element_type=jnp.float32,
    )
    second = mine + coarse_step * (rhs_ref[...] - applied) / dc_ref[...]
    for i in range(second_ref.shape[0]):
        second_ref[i] = second


def middle_kernel(shape, second_ref, dc_ref, *refs):
    faces, (u1, owners, scale, u2, u5, rhs_ref, first_ref, u3, u4, moves, acc) = refs[:6], refs[6:]
    s = shape
    slab = lax.axis_index("slab")
    row = lax.axis_index("row")
    fields = Fields(s, faces, u1)
    layers = NEED - 1

    def correct(z, lo, hi):
        dz = (z + s.oz) // s.cz - s.reach
        for dy in (-1, 0, 1):
            begin, end = max(lo, dy * s.cy), min(hi, (dy + 1) * s.cy)
            if begin >= end:
                continue
            p = jnp.clip(slab + dz, 0, s.n_slab - 1)
            q = jnp.clip(row + dy, 0, s.n_row - 1)
            at = s.oy + dy * s.cy
            spread(second_ref, p * s.n_row + q, owners[z + s.oz, at : at + s.cy], moves, z + layers, at)
        for y in range(lo, hi):
            u4[z + layers, y + layers] = u2[z + layers, y + layers] + moves[z + layers, y + s.oy]

    fields.region(layers, correct)
    fields.sweep(u4, layers, u3, layers, layers - 1)
    fields.sweep(u3, layers, u4, layers, layers - 2)
    fields.sweep(u4, layers, u5, 1, 1)
    rhs = fields.coarse_sums(u5, 1, scale, owners, acc)
    rhs_ref[...] = rhs
    first = coarse_step * rhs / dc_ref[...]
    for t in range(s.group):
        first_ref[t] = first


def last_kernel(shape, own_ref, z0, z1, y0, y1, *refs):
    faces, (u1, owners, u5, out_ref, u6, tables) = refs[:6], refs[6:]
    s = shape
    slab = lax.axis_index("slab")
    row = lax.axis_index("row")
    fields = Fields(s, faces, u1)

    def pick(even, first, second):
        return jnp.where(even, first[0], second[0])

    tables[0] = own_ref[0]
    tables[1] = pick(slab % 2 == 0, z0, z1)
    tables[2] = pick(slab % 2 == 0, z1, z0)
    up_y = pick(row % 2 == 0, y0, y1)
    down_y = pick(row % 2 == 0, y1, y0)
    for z in range(-1, s.cz + 1):
        index = 2 if z < 0 else 1 if z == s.cz else 0
        spread(tables, index, owners[z + s.oz, s.oy : s.oy + s.cy], u6, z + 1, 1)
        for y in range(s.cy):
            u6[z + 1, y + 1] += u5[z + 1, y + 1]
        if index == 0:
            for y, tab in ((-1, down_y), (s.cy, up_y)):
                ids = owners[z + s.oz, y + s.oy : y + s.oy + 1, :]
                u6[z + 1, y + 1] = u5[z + 1, y + 1] + take(tab, ids, s)

    def body(z, lo, hi):
        def use(y, centre, total):
            out_ref[:, z, y, :] = (1.0 - smooth_step) * centre + total

        fields.moved_rows(u6, 1, z, lo, hi, use)

    fields.region(0, body)


def f32(*dims):
    return jax.ShapeDtypeStruct(dims, jnp.float32)


def i32(*dims):
    return jax.ShapeDtypeStruct(dims, jnp.int32)


def per_device(edge_weights, seeds, supervoxel, coarse_blocks):
    s = Shape(edge_weights, coarse_blocks)
    messages = []
    for d in s.partial:
        count = max(len(items) for items in s.plane_items(d))
        messages += [i32(count, s.cy, s.nx)] * 2
    own, blocks, *messages = pl.pallas_call(
        functools.partial(start_kernel, s),
        out_shape=tuple(
            [i32(ARRAYS * s.cz, s.cy, s.nx), f32(*coarse_blocks.shape[1:])] + messages
        ),
        in_specs=[pl.BlockSpec(memory_space=pltpu.HBM)] * 4,
        out_specs=tuple(vmem(2 + len(messages))),
        scratch_shapes=[pltpu.SemaphoreType.DMA((ARRAYS + 1,))],
        compiler_params=params(),
        name="start",
    )(*[pltpu.with_memory_space_constraint(x, pltpu.HBM) for x in (edge_weights, seeds, supervoxel, coarse_blocks[0])])
    recvs = []
    for d in range(1, s.reach + 1):
        for ph in (0, 1):
            sent = messages[2 * s.partial.index(d) + ph] if d in s.partial else own
            recvs.append(swap(sent, "slab", d, ph))
    rows = -(-max(s.row_items(0)[1], s.row_items(1)[1]) // 8) * 8
    frame, even, odd, dc = pl.pallas_call(
        functools.partial(pack_kernel, s),
        out_shape=(
            i32(ARRAYS, s.planes, s.cy, s.nx),
            i32(rows, s.nx),
            i32(rows, s.nx),
            f32(1, s.cc),
        ),
        in_specs=vmem(2 + len(recvs)),
        out_specs=tuple(vmem(4)),
        compiler_params=params(),
        name="pack",
    )(own, blocks, *recvs)
    even = swap(even, "row", 1, 0)
    odd = swap(odd, "row", 1, 1)
    plane = (s.planes, s.rows, s.nx)
    wide = 2 * (NEED - 1)
    *faces, u1, owners, scale, u2, rhs, first = pl.pallas_call(
        functools.partial(down_kernel, s),
        out_shape=tuple(
            [f32(*plane)] * 6
            + [f32(s.cz + 2 * NEED, s.cy + 2 * NEED, LABELS, s.nx), i32(*plane)]
            + [f32(s.cz, s.rows, s.nx), f32(s.cz + wide, s.cy + wide, LABELS, s.nx)]
            + [f32(LABELS, s.cc), f32(s.group, LABELS, s.cc)]
        ),
        in_specs=vmem(4),
        out_specs=tuple(vmem(12)),
        scratch_shapes=[
            pltpu.VMEM(plane, jnp.float32),
            pltpu.VMEM((ARRAYS,) + plane, jnp.int32),
            pltpu.VMEM((3 * LABELS, s.cc), jnp.float32),
        ],
        compiler_params=params(),
        name="down",
    )(frame, even, odd, dc)

    groups = [[t * s.sections + g for t in range(s.group)] for g in range(s.sections)]

    def coarse(first, rhs, copies):
        gathered = lax.all_to_all(
            first, "slab", 0, 0, axis_index_groups=groups if s.sections > 1 else None, tiled=True
        )
        return pl.pallas_call(
            functools.partial(coarse_kernel, s),
            out_shape=f32(copies, LABELS, s.cc),
            in_specs=vmem(4),
            out_specs=vmem(1)[0],
            compiler_params=params(),
            name="coarse",
        )(gathered, rhs, blocks, dc)

    second = coarse(first, rhs, s.n_slab * s.n_row)
    second = lax.all_to_all(second, BOTH, 0, 0, tiled=True)
    u5, rhs, first = pl.pallas_call(
        functools.partial(middle_kernel, s),
        out_shape=(
            f32(s.cz + 2, s.cy + 2, LABELS, s.nx),
            f32(LABELS, s.cc),
            f32(s.group, LABELS, s.cc),
        ),
        in_specs=vmem(12),
        out_specs=tuple(vmem(3)),
        scratch_shapes=[
            pltpu.VMEM((s.cz + wide, s.cy + wide, LABELS, s.nx), jnp.float32),
            pltpu.VMEM((s.cz + wide, s.cy + wide, LABELS, s.nx), jnp.float32),
            pltpu.VMEM((s.cz + wide, s.rows, LABELS, s.nx), jnp.float32),
            pltpu.VMEM((3 * LABELS, s.cc), jnp.float32),
        ],
        compiler_params=params(),
        name="middle",
    )(second, dc, *faces, u1, owners, scale, u2)
    second = coarse(first, rhs, 1)
    around = [swap(second, axis, 1, ph) for axis in ("slab", "row") for ph in (0, 1)]
    return pl.pallas_call(
        functools.partial(last_kernel, s),
        out_shape=f32(LABELS, s.cz, s.cy, s.nx),
        in_specs=vmem(14),
        out_specs=vmem(1)[0],
        scratch_shapes=[
            pltpu.VMEM((s.cz + 2, s.cy + 2, LABELS, s.nx), jnp.float32),
            pltpu.VMEM((3, LABELS, s.cc), jnp.float32),
        ],
        compiler_params=params(),
        name="last",
    )(second, *around, *faces, u1, owners, u5)


def solution(mesh):
    in_specs = (
        P(None, "slab", "row", None),
        P("slab", "row", None),
        P("slab", "row", None),
        P("row", "slab", None),
    )
    out_specs = P(None, "slab", "row", None)
    return jax.shard_map(
        per_device, mesh=mesh, in_specs=in_specs, out_specs=out_specs, check_vma=False
    )
```

```python
import functools

import jax
import jax.numpy as jnp
from jax import lax
from jax.experimental import pallas as pl
from jax.experimental.pallas import tpu as pltpu
from jax.sharding import PartitionSpec as P

LABELS = 8
ARRAYS = 5

prior_mass = 0.25
seed_weight = 4.0
smooth_step = 0.8
coarse_step = 0.7
weight_unit = 0.125

BOTH = ("slab", "row")
NEED = 5
VMEM_LIMIT = 24 * 1024 * 1024


def pairing(n_slab, n_row, axis, distance, phase):
    count = n_slab if axis == "slab" else n_row
    spare = n_row if axis == "slab" else n_slab
    pairs = []
    for s in range(n_slab):
        for r in range(n_row):
            i, other = (s, r) if axis == "slab" else (r, s)
            if (i // distance) % 2 == phase and i + distance < count:
                j, k = i + distance, other
            elif i >= distance and (i // distance - 1) % 2 == phase:
                j, k = i - distance, other
            elif spare % 2 == 0:
                j, k = i, other ^ 1
            else:
                continue
            target = (j, k) if axis == "slab" else (k, j)
            pairs.append((s * n_row + r, target[0] * n_row + target[1]))
    return pairs


def swap(block, axis, distance, phase):
    n_slab, n_row = lax.axis_size("slab"), lax.axis_size("row")
    return lax.ppermute(block, BOTH, pairing(n_slab, n_row, axis, distance, phase))


def vmem(count):
    return [pl.BlockSpec(memory_space=pltpu.VMEM)] * count


def params():
    return pltpu.CompilerParams(vmem_limit_bytes=VMEM_LIMIT)


class Shape:
    def __init__(self, edge_weights, coarse_blocks):
        self.cz, self.cy, self.nx = edge_weights.shape[1:]
        self.cc = coarse_blocks.shape[1]
        self.group = coarse_blocks.shape[2] // self.cc
        self.n_slab = lax.axis_size("slab")
        self.n_row = lax.axis_size("row")
        self.sections = self.n_slab // self.group
        self.reach = -(-(NEED + 1) // self.cz)
        self.oz = self.reach * self.cz
        self.planes = self.cz + 2 * self.oz
        self.rows = 3 * self.cy
        self.oy = self.cy
        full = ARRAYS * self.cz
        self.partial = [
            d for d in range(1, self.reach + 1) if min(map(len, self.plane_items(d))) < full
        ]

    def away(self, z):
        return -z if z < 0 else max(0, z - self.cz + 1)

    def needed(self, z):
        base = NEED - self.away(z)
        next_plane = 1 if z < 0 else 0
        below = (base + next_plane, base + 1, base, base, base - 1)
        above = (base + next_plane, base, base, base, base - 1)
        return [(max(-1, lo), max(-1, hi)) for lo, hi in zip(below, above)]

    def plane_items(self, distance):
        items = [(a, z) for a in range(ARRAYS) for z in range(self.cz)]
        shift = distance * self.cz
        up = [(a, z) for a, z in items if self.wanted(a, z - shift) >= 0]
        down = [(a, z) for a, z in items if self.wanted(a, z + shift) >= 0]
        return up, down

    def wanted(self, a, z):
        base = NEED - self.away(z)
        return (base + (1 if z < 0 else 0), base, base, base, base - 1)[a]

    def group_planes(self, group):
        planes = range(-self.oz, self.cz + self.oz)
        return [z for z in planes if (-self.cz <= z < 2 * self.cz) == (group == 0)]

    def row_items(self, side, group):
        out, at = [], 0
        for z in self.group_planes(group):
            for a, counts in enumerate(self.needed(z)):
                if counts[side] > 0:
                    out.append((a, z, at, counts[side]))
                    at += counts[side]
        return out, at


def parity_of(index, distance):
    return (index // distance) % 2


def start_kernel(shape, edge_ref, seeds_ref, owners_ref, blocks_in, own_ref, blocks_ref, *refs):
    sems = refs[-1]
    cz = shape.cz
    copies = [
        pltpu.make_async_copy(source, own_ref.at[pl.ds(a * cz, cz)], sems.at[a])
        for a, source in enumerate([edge_ref.at[0], edge_ref.at[1], edge_ref.at[2], seeds_ref, owners_ref])
    ]
    fetch = pltpu.make_async_copy(blocks_in, blocks_ref, sems.at[ARRAYS])
    for copy in copies:
        copy.start()
    fetch.start()
    for copy in copies:
        copy.wait()
    slab = lax.axis_index("slab")
    for i, d in enumerate(shape.partial):
        first_ref, second_ref = refs[2 * i], refs[2 * i + 1]
        up, down = shape.plane_items(d)

        def fill(up_ref, down_ref, up=up, down=down):
            for items, ref in ((up, up_ref), (down, down_ref)):
                for n in range(ref.shape[0]):
                    a, z = items[min(n, len(items) - 1)]
                    ref[n] = own_ref[a * cz + z]

        @pl.when(parity_of(slab, d) == 0)
        def _():
            fill(first_ref, second_ref)

        @pl.when(parity_of(slab, d) == 1)
        def _():
            fill(second_ref, first_ref)

    fetch.wait()


def pack_kernel(shape, group, *refs):
    s = shape
    distances = [1] if group == 0 else list(range(2, s.reach + 1))
    outs = 4 if group == 0 else 3
    ins, (frame_ref, even_ref, odd_ref, *more) = refs[:-outs], refs[-outs:]
    slab = lax.axis_index("slab")
    row = lax.axis_index("row")
    cz, oz = s.cz, s.oz
    if group == 0:
        own_ref, blocks_ref, *recvs = ins
        for a in range(ARRAYS):
            for z in range(cz):
                frame_ref[a, oz + z] = own_ref[a * cz + z]
    else:
        recvs = ins
    for n, d in enumerate(distances):
        first, second = recvs[2 * n], recvs[2 * n + 1]
        up, down = s.plane_items(d)

        def place(above, below, d=d, up=up, down=down):
            for n, (a, z) in enumerate(down):
                frame_ref[a, oz + d * cz + z] = above[n]
            for n, (a, z) in enumerate(up):
                frame_ref[a, oz - d * cz + z] = below[n]

        @pl.when(parity_of(slab, d) == 0)
        def _():
            place(first, second)

        @pl.when(parity_of(slab, d) == 1)
        def _():
            place(second, first)

    def fill(last_ref, first_ref):
        for a, z, at, count in s.row_items(0, group)[0]:
            last_ref[at : at + count] = frame_ref[a, oz + z, s.cy - count :]
        for a, z, at, count in s.row_items(1, group)[0]:
            first_ref[at : at + count] = frame_ref[a, oz + z, :count]

    @pl.when(row % 2 == 0)
    def _():
        fill(even_ref, odd_ref)

    @pl.when(row % 2 == 1)
    def _():
        fill(odd_ref, even_ref)

    if group == 0:
        turn = slab // s.sections
        block = blocks_ref[:, pl.ds(pl.multiple_of(turn * s.cc, s.cc), s.cc)]
        a = lax.broadcasted_iota(jnp.int32, block.shape, 0)
        b = lax.broadcasted_iota(jnp.int32, block.shape, 1)
        more[0][...] = jnp.sum(jnp.where(a == b, block, 0.0), axis=0, keepdims=True)


def row_of(ref, z, y, count):
    return jnp.broadcast_to(ref[z, y : y + 1, :], (LABELS, count))


class Fields:
    def __init__(self, shape, faces, u1):
        self.s, self.faces, self.u1 = shape, faces, u1

    def region(self, layers, body):
        s = self.s
        for z in range(-layers, s.cz + layers):
            reach = layers - s.away(z)
            body(z, -reach, s.cy + reach)

    def moved_rows(self, src, at, z, lo, hi, use):
        s = self.s
        zz, z, z1 = z + s.oz, z + at, z + NEED
        before = src[z, lo - 1 + at]
        centre = src[z, lo + at]
        for y in range(lo, hi):
            above_z, below_z, above_y, below_y, above_x, below_x = [
                row_of(face, zz, y + s.oy, s.nx) for face in self.faces
            ]
            after = src[z, y + 1 + at]
            total = above_x * pltpu.roll(centre, s.nx - 1, axis=1)
            total += below_x * pltpu.roll(centre, 1, axis=1)
            total += above_y * after + below_y * before
            total += above_z * src[z + 1, y + at] + below_z * src[z - 1, y + at]
            use(y, centre, total + self.u1[z1, y + NEED])
            before, centre = centre, after

    def sweep(self, src, src_at, dst, dst_at, layers):
        def body(z, lo, hi):
            def use(y, centre, total):
                dst[z + dst_at, y + dst_at] = (1.0 - smooth_step) * centre + total

            self.moved_rows(src, src_at, z, lo, hi, use)

        self.region(layers, body)

    def coarse_sums(self, src, src_at, scale, owners, acc):
        s = self.s
        acc[...] = jnp.zeros_like(acc)
        pack = 16
        cells = lax.broadcasted_iota(jnp.int32, (s.cc, s.nx), 0).astype(jnp.float32)
        cells = cells.astype(jnp.bfloat16).reshape(s.cc // pack, pack, s.nx)
        one, none = jnp.bfloat16(1), jnp.bfloat16(0)

        def body(z, lo, hi):
            def use(y, centre, total):
                rest = row_of(scale, z, y + s.oy, s.nx) * (total - smooth_step * centre)
                top = rest.astype(jnp.bfloat16).astype(jnp.float32)
                mid = (rest - top).astype(jnp.bfloat16).astype(jnp.float32)
                low = rest - top - mid
                parts = jnp.concatenate([top, mid, low], axis=0).astype(jnp.bfloat16)
                ids = owners[z + s.oz, y + s.oy : y + s.oy + 1, :].astype(jnp.float32)
                ids = jnp.broadcast_to(ids, (pack, s.nx)).astype(jnp.bfloat16)
                onehot = jnp.where(ids[None] == cells, one, none).reshape(s.cc, s.nx)
                acc[...] += lax.dot_general(
                    parts, onehot, (((1,), (1,)), ((), ())), preferred_element_type=jnp.float32
                )

            self.moved_rows(src, src_at, z, lo, hi, use)

        self.region(0, body)
        return acc[0:LABELS] + acc[LABELS : 2 * LABELS] + acc[2 * LABELS : 3 * LABELS]


def take(table, ids, shape):
    ids = jnp.broadcast_to(ids, (LABELS, shape.nx))
    numbers = lax.GatherDimensionNumbers(
        offset_dims=(),
        collapsed_slice_dims=(1,),
        start_index_map=(1,),
        operand_batching_dims=(0,),
        start_indices_batching_dims=(0,),
    )
    parts = [
        lax.gather(
            table,
            ids[:, i : i + shape.cc, None],
            numbers,
            (1, 1),
            mode=lax.GatherScatterMode.PROMISE_IN_BOUNDS,
        )
        for i in range(0, shape.nx, shape.cc)
    ]
    return jnp.concatenate(parts, axis=1)


def spread(tables, index, ids, dst, z, y):
    numbers = lax.GatherDimensionNumbers(
        offset_dims=(),
        collapsed_slice_dims=(1,),
        start_index_map=(1,),
        operand_batching_dims=(0,),
        start_indices_batching_dims=(0,),
    )
    count, width = ids.shape
    lanes = tables.shape[2]
    for x in range(0, width, lanes):
        part = ids[:, x : x + lanes, None]
        for l in range(LABELS):
            row = jnp.broadcast_to(tables[index, l : l + 1, :], (count, lanes))
            dst[z, y : y + count, l, x : x + lanes] = lax.gather(
                row, part, numbers, (1, 1), mode=lax.GatherScatterMode.PROMISE_IN_BOUNDS
            )


def down_kernel(shape, near_ref, even0, odd0, far_ref, even1, odd1, dc_ref, *refs):
    faces, (u1, owners, scale, u2, rhs_ref, first_ref, kept, ints, acc) = refs[:6], refs[6:]
    s = shape
    slab = lax.axis_index("slab")
    row = lax.axis_index("row")
    cz, cy, oy, oz = s.cz, s.cy, s.oy, s.oz

    def sides(group, below_ref, above_ref):
        for a, z, at, count in s.row_items(0, group)[0]:
            ints[a, oz + z, oy - count : oy] = below_ref[at : at + count]
        for a, z, at, count in s.row_items(1, group)[0]:
            ints[a, oz + z, oy + cy : oy + cy + count] = above_ref[at : at + count]

    @pl.when(row % 2 == 0)
    def _():
        sides(0, odd0, even0)
        sides(1, odd1, even1)

    @pl.when(row % 2 == 1)
    def _():
        sides(0, even0, odd0)
        sides(1, even1, odd1)

    labels = lax.broadcasted_iota(jnp.int32, (LABELS, s.nx), 0)
    line = row * cy - oy + lax.broadcasted_iota(jnp.int32, (s.rows, s.nx), 0)
    column = lax.broadcasted_iota(jnp.int32, (s.rows, s.nx), 1)
    inside_y = jnp.logical_and(line >= 0, line < cy * s.n_row)
    unit_y = jnp.where(jnp.logical_and(line != -1, line != cy * s.n_row - 1), weight_unit, 0.0)
    unit_x = jnp.where(column < s.nx - 1, weight_unit, 0.0)

    def weights_z(i):
        plane = slab * cz + i - oz
        inside = jnp.logical_and(plane != -1, plane != cz * s.n_slab - 1)
        return ints[0, i].astype(jnp.float32) * jnp.where(inside, weight_unit, 0.0)

    near = [oz + z for z in s.group_planes(0)]

    def centre(a, i):
        ints[a, i, oy : oy + cy] = (near_ref if i in near else far_ref)[a, i]

    def prepare(i, below_z):
        for a in range(ARRAYS):
            centre(a, i)
        w_z = weights_z(i)
        w_y = ints[1, i].astype(jnp.float32) * unit_y
        w_x = ints[2, i].astype(jnp.float32) * unit_x
        below_y = pltpu.roll(w_y, 1, axis=0)
        below_x = pltpu.roll(w_x, 1, axis=1)
        seeded = jnp.where(ints[3, i] >= 0, seed_weight + prior_mass, prior_mass)
        d = seeded + w_z + w_y + w_x + below_z + below_y + below_x
        plane = slab * cz + i - oz
        inside_z = jnp.logical_and(plane >= 0, plane < cz * s.n_slab)
        inside = jnp.logical_and(inside_y, inside_z)
        k = jnp.where(inside, smooth_step / d, 0.0)
        for face, w in zip(faces, (w_z, below_z, w_y, below_y, w_x, below_x)):
            face[i] = k * w
        kept[i] = seed_weight * k
        owners[i] = jnp.where(inside, ints[4, i], 0)

        if oz <= i < oz + cz:
            scale[i - oz] = d / smooth_step
        return w_z

    centre(0, 0)
    below = weights_z(0)
    for i in range(1, s.planes - 1):
        below = prepare(i, below)
    fields = Fields(s, faces, u1)

    def start(z, lo, hi):
        for y in range(lo, hi):
            seed = jnp.broadcast_to(ints[3, z + oz, y + oy : y + oy + 1, :], (LABELS, s.nx))
            value = row_of(kept, z + oz, y + oy, s.nx)
            u1[z + NEED, y + NEED] = jnp.where(seed == labels, value, 0.0)

    fields.region(NEED, start)
    fields.sweep(u1, NEED, u2, NEED - 1, NEED - 1)
    rhs = fields.coarse_sums(u2, NEED - 1, scale, owners, acc)
    rhs_ref[...] = rhs
    first = coarse_step * rhs / dc_ref[...]
    for t in range(s.group):
        first_ref[t] = first


def coarse_kernel(shape, first_ref, rhs_ref, blocks_ref, dc_ref, second_ref):
    s = shape
    turn = lax.axis_index("slab") // s.sections
    mine = first_ref[turn]
    whole = jnp.concatenate([first_ref[t] for t in range(s.group)], axis=1)
    applied = lax.dot_general(
        whole,
        blocks_ref[...],
        (((1,), (1,)), ((), ())),
        precision=lax.Precision.HIGHEST,
        preferred_element_type=jnp.float32,
    )
    second = mine + coarse_step * (rhs_ref[...] - applied) / dc_ref[...]
    for i in range(second_ref.shape[0]):
        second_ref[i] = second


def middle_kernel(shape, second_ref, dc_ref, *refs):
    faces, (u1, owners, scale, u2, u5, rhs_ref, first_ref, u3, u4, moves, acc) = refs[:6], refs[6:]
    s = shape
    slab = lax.axis_index("slab")
    row = lax.axis_index("row")
    fields = Fields(s, faces, u1)
    layers = NEED - 1

    def correct(z, lo, hi):
        dz = (z + s.oz) // s.cz - s.reach
        for dy in (-1, 0, 1):
            begin, end = max(lo, dy * s.cy), min(hi, (dy + 1) * s.cy)
            if begin >= end:
                continue
            p = jnp.clip(slab + dz, 0, s.n_slab - 1)
            q = jnp.clip(row + dy, 0, s.n_row - 1)
            at = s.oy + dy * s.cy
            spread(second_ref, p * s.n_row + q, owners[z + s.oz, at : at + s.cy], moves, z + layers, at)
        for y in range(lo, hi):
            u4[z + layers, y + layers] = u2[z + layers, y + layers] + moves[z + layers, y + s.oy]

    fields.region(layers, correct)
    fields.sweep(u4, layers, u3, layers, layers - 1)
    fields.sweep(u3, layers, u4, layers, layers - 2)
    fields.sweep(u4, layers, u5, 1, 1)
    rhs = fields.coarse_sums(u5, 1, scale, owners, acc)
    rhs_ref[...] = rhs
    first = coarse_step * rhs / dc_ref[...]
    for t in range(s.group):
        first_ref[t] = first


def last_kernel(shape, own_ref, z0, z1, y0, y1, *refs):
    faces, (u1, owners, u5, out_ref, u6, tables) = refs[:6], refs[6:]
    s = shape
    slab = lax.axis_index("slab")
    row = lax.axis_index("row")
    fields = Fields(s, faces, u1)

    def pick(even, first, second):
        return jnp.where(even, first[0], second[0])

    tables[0] = own_ref[0]
    tables[1] = pick(slab % 2 == 0, z0, z1)
    tables[2] = pick(slab % 2 == 0, z1, z0)
    up_y = pick(row % 2 == 0, y0, y1)
    down_y = pick(row % 2 == 0, y1, y0)
    for z in range(-1, s.cz + 1):
        index = 2 if z < 0 else 1 if z == s.cz else 0
        spread(tables, index, owners[z + s.oz, s.oy : s.oy + s.cy], u6, z + 1, 1)
        for y in range(s.cy):
            u6[z + 1, y + 1] += u5[z + 1, y + 1]
        if index == 0:
            for y, tab in ((-1, down_y), (s.cy, up_y)):
                ids = owners[z + s.oz, y + s.oy : y + s.oy + 1, :]
                u6[z + 1, y + 1] = u5[z + 1, y + 1] + take(tab, ids, s)

    def body(z, lo, hi):
        def use(y, centre, total):
            out_ref[:, z, y, :] = (1.0 - smooth_step) * centre + total

        fields.moved_rows(u6, 1, z, lo, hi, use)

    fields.region(0, body)


def f32(*dims):
    return jax.ShapeDtypeStruct(dims, jnp.float32)


def i32(*dims):
    return jax.ShapeDtypeStruct(dims, jnp.int32)


def per_device(edge_weights, seeds, supervoxel, coarse_blocks):
    s = Shape(edge_weights, coarse_blocks)
    messages = []
    for d in s.partial:
        count = max(len(items) for items in s.plane_items(d))
        messages += [i32(count, s.cy, s.nx)] * 2
    own, blocks, *messages = pl.pallas_call(
        functools.partial(start_kernel, s),
        out_shape=tuple(
            [i32(ARRAYS * s.cz, s.cy, s.nx), f32(*coarse_blocks.shape[1:])] + messages
        ),
        in_specs=[pl.BlockSpec(memory_space=pltpu.HBM)] * 4,
        out_specs=tuple(vmem(2 + len(messages))),
        scratch_shapes=[pltpu.SemaphoreType.DMA((ARRAYS + 1,))],
        compiler_params=params(),
        name="start",
    )(*[pltpu.with_memory_space_constraint(x, pltpu.HBM) for x in (edge_weights, seeds, supervoxel, coarse_blocks[0])])
    recvs = []
    for d in range(1, s.reach + 1):
        for ph in (0, 1):
            sent = messages[2 * s.partial.index(d) + ph] if d in s.partial else own
            recvs.append(swap(sent, "slab", d, ph))

    def pack(group, *operands):
        rows = -(-max(s.row_items(0, group)[1], s.row_items(1, group)[1]) // 8) * 8
        shapes = [i32(ARRAYS, s.planes, s.cy, s.nx), i32(rows, s.nx), i32(rows, s.nx)]
        shapes += [f32(1, s.cc)] * (group == 0)
        frame, even, odd, *more = pl.pallas_call(
            functools.partial(pack_kernel, s, group),
            out_shape=tuple(shapes),
            in_specs=vmem(len(operands)),
            out_specs=tuple(vmem(len(shapes))),
            compiler_params=params(),
        )(*operands)
        odd = swap(odd, "row", 1, 1)
        even = swap(even, "row", 1, 0)
        return [frame, even, odd], more

    near, (dc,) = pack(0, own, blocks, *recvs[:2])
    far, _ = pack(1, *recvs[2:])
    plane = (s.planes, s.rows, s.nx)
    wide = 2 * (NEED - 1)
    *faces, u1, owners, scale, u2, rhs, first = pl.pallas_call(
        functools.partial(down_kernel, s),
        out_shape=tuple(
            [f32(*plane)] * 6
            + [f32(s.cz + 2 * NEED, s.cy + 2 * NEED, LABELS, s.nx), i32(*plane)]
            + [f32(s.cz, s.rows, s.nx), f32(s.cz + wide, s.cy + wide, LABELS, s.nx)]
            + [f32(LABELS, s.cc), f32(s.group, LABELS, s.cc)]
        ),
        in_specs=vmem(7),
        out_specs=tuple(vmem(12)),
        scratch_shapes=[
            pltpu.VMEM(plane, jnp.float32),
            pltpu.VMEM((ARRAYS,) + plane, jnp.int32),
            pltpu.VMEM((3 * LABELS, s.cc), jnp.float32),
        ],
        compiler_params=params(),
        name="down",
    )(*near, *far, dc)

    groups = [[t * s.sections + g for t in range(s.group)] for g in range(s.sections)]

    def coarse(first, rhs, copies):
        gathered = lax.all_to_all(
            first, "slab", 0, 0, axis_index_groups=groups if s.sections > 1 else None, tiled=True
        )
        return pl.pallas_call(
            functools.partial(coarse_kernel, s),
            out_shape=f32(copies, LABELS, s.cc),
            in_specs=vmem(4),
            out_specs=vmem(1)[0],
            compiler_params=params(),
            name="coarse",
        )(gathered, rhs, blocks, dc)

    second = coarse(first, rhs, s.n_slab * s.n_row)
    second = lax.all_to_all(second, BOTH, 0, 0, tiled=True)
    u5, rhs, first = pl.pallas_call(
        functools.partial(middle_kernel, s),
        out_shape=(
            f32(s.cz + 2, s.cy + 2, LABELS, s.nx),
            f32(LABELS, s.cc),
            f32(s.group, LABELS, s.cc),
        ),
        in_specs=vmem(12),
        out_specs=tuple(vmem(3)),
        scratch_shapes=[
            pltpu.VMEM((s.cz + wide, s.cy + wide, LABELS, s.nx), jnp.float32),
            pltpu.VMEM((s.cz + wide, s.cy + wide, LABELS, s.nx), jnp.float32),
            pltpu.VMEM((s.cz + wide, s.rows, LABELS, s.nx), jnp.float32),
            pltpu.VMEM((3 * LABELS, s.cc), jnp.float32),
        ],
        compiler_params=params(),
        name="middle",
    )(second, dc, *faces, u1, owners, scale, u2)
    second = coarse(first, rhs, 1)
    around = [swap(second, axis, 1, ph) for axis in ("slab", "row") for ph in (0, 1)]
    return pl.pallas_call(
        functools.partial(last_kernel, s),
        out_shape=f32(LABELS, s.cz, s.cy, s.nx),
        in_specs=vmem(14),
        out_specs=vmem(1)[0],
        scratch_shapes=[
            pltpu.VMEM((s.cz + 2, s.cy + 2, LABELS, s.nx), jnp.float32),
            pltpu.VMEM((3, LABELS, s.cc), jnp.float32),
        ],
        compiler_params=params(),
        name="last",
    )(second, *around, *faces, u1, owners, u5)


def solution(mesh):
    in_specs = (
        P(None, "slab", "row", None),
        P("slab", "row", None),
        P("slab", "row", None),
        P("row", "slab", None),
    )
    out_specs = P(None, "slab", "row", None)
    return jax.shard_map(
        per_device, mesh=mesh, in_specs=in_specs, out_specs=out_specs, check_vma=False
    )
```
